512 devices in a mesh: row: 32 (over x, y), col: 16 (over z, core).
Axes of the slice: x: 4, y: 8, z: 8, core: 2. Of those that a mesh axis runs over, the one named last changes fastest.
Arguments:
- points_here: float32 [4, 3, 128, 256, 128], P(None, None, 'row', 'col'), may hold values from -4 to 4
- points_there: float32 [4, 3, 128, 256, 128], P(None, None, 'row', 'col'), may hold values from -4 to 4
- outlier_mask: int32 [4, 128, 256, 128], P(None, 'row', 'col'), may hold values 0 or 1
- transforms: float32 [3, 4, 128, 256], P(None, None, 'row', 'col'), may hold values from -3 to 3
Outputs:
- aligned: float32 [3, 4, 128, 256], P(None, None, 'row', 'col')
- error_stats: float32 [2, 2], replicated
The draws below stay inside these ranges and needn't reach their ends.
All inputs are finite; a program needn't handle non-finite values. No bound on the sum of `outlier_mask` on one device may be relied on, other than what follows from the above.
Results may differ from the reference program's by a relative error of at most 0.0003.
Values sent between devices are 32-bit elements; how exact they have to be, the bound alone decides.
A program may use at most 64 MiB of HBM per device.

```python
import jax
import jax.numpy as jnp
from jax import lax

PAIRS = 128
LINKS = 4
ITERS = 2
GR = 128
GC = 256


def set_ends(array, rng, smallest, high):
    shape = array.shape
    place = [jax.random.randint(jax.random.fold_in(rng, axis), (), 0, shape[axis]) for axis in range(len(shape))]
    array = array.at[tuple(place)].set(smallest)
    longest = shape.index(max(shape))
    place[longest] = (place[longest] + 1) % shape[longest]
    return array.at[tuple(place)].set(high)


def block_levels(rng, extent, pieces, smallest, top_value):
    gain = 1.0
    for position, parts in pieces:
        heights = jax.random.uniform(jax.random.fold_in(jax.random.fold_in(rng, 6), position), (parts,), jnp.float32, smallest / len(pieces), top_value / len(pieces))
        gain = gain * jnp.repeat(jnp.exp(heights), extent[position] // parts).reshape((-1,) + (1,) * (len(extent) - 1 - position))
    return gain


def bell_draw(key, extent, deviation, limit, split=(), kind=jnp.bfloat16):
    drawn = jax.random.normal(key, extent, jnp.float32) * deviation
    if len(split) > 0:
        drawn = block_levels(key, extent, split, -0.22, 0.18) * drawn
    return jnp.clip(drawn, min=-limit, max=limit).astype(kind)


def setup_inputs(seed: int = 0) -> dict:
    streams_of = jax.random.split(jax.random.key(seed), 5)
    points_here = bell_draw(streams_of[0], (LINKS, 3, GR, GC, PAIRS), 1.0, 4.0, ((2, 32), (3, 16)), jnp.float32)
    points_there = bell_draw(streams_of[1], (LINKS, 3, GR, GC, PAIRS), 1.0, 4.0, ((2, 32), (3, 16)), jnp.float32)
    outlier_mask = set_ends((jax.random.randint(streams_of[2], (LINKS, GR, GC, PAIRS), 0, 4) < 3).astype(jnp.int32), jax.random.fold_in(streams_of[2], 1), 0, 1)
    transforms = bell_draw(streams_of[3], (3, 4, GR, GC), 0.5, 3.0, ((2, 32), (3, 16)), jnp.float32)
    return dict(points_here=points_here, points_there=points_there, outlier_mask=outlier_mask, transforms=transforms)


link_offsets = ((0, 1), (1, 0), (1, 1), (1, -1))
damping_scale = 64.0

def apply_affine(affine, points):
    mapped = []
    for component in range(3):
        value = affine[component, 3][..., None] + affine[component, 0][..., None] * points[0]
        value = value + affine[component, 1][..., None] * points[1]
        value = value + affine[component, 2][..., None] * points[2]
        mapped.append(value)
    return jnp.stack(mapped)

def link_error(here, there):
    delta = here - there
    return delta[0] * delta[0] + delta[1] * delta[1] + delta[2] * delta[2]

def gram_terms(weight, points):
    weighted = [weight * points[0], weight * points[1], weight * points[2], weight]
    entries = []
    for first in range(4):
        for second in range(4):
            if second == 3:
                entries.append(lax.optimization_barrier(jnp.sum(weighted[first], axis=-1)))
            else:
                entries.append(lax.optimization_barrier(jnp.sum(weighted[first] * points[second], axis=-1)))
    return jnp.stack(entries).reshape((4, 4) + weight.shape[:-1])

def cross_terms(weight, target, points):
    entries = []
    for component in range(3):
        scaled = weight * target[component]
        for second in range(4):
            if second == 3:
                entries.append(lax.optimization_barrier(jnp.sum(scaled, axis=-1)))
            else:
                entries.append(lax.optimization_barrier(jnp.sum(scaled * points[second], axis=-1)))
    return jnp.stack(entries).reshape((3, 4) + weight.shape[:-1])

def solve_small(gram, rhs):
    factor = [[None] * 4 for _ in range(4)]
    for first in range(4):
        for second in range(first + 1):
            value = gram[first, second]
            for inner in range(second):
                value = value - factor[first][inner] * factor[second][inner]
            if first == second:
                factor[first][first] = jnp.sqrt(value)
            else:
                factor[first][second] = value / factor[second][second]
    result = []
    for component in range(3):
        forward = []
        for first in range(4):
            value = rhs[component, first]
            for inner in range(first):
                value = value - factor[first][inner] * forward[inner]
            forward.append(value / factor[first][first])
        backward = [None] * 4
        for first in (3, 2, 1, 0):
            value = forward[first]
            for inner in range(first + 1, 4):
                value = value - factor[inner][first] * backward[inner]
            backward[first] = value / factor[first][first]
        result.append(jnp.stack(backward))
    return jnp.stack(result)

def neighbour_of(affine, row_step, col_step):
    padded = jnp.pad(affine, ((0, 0), (0, 0), (0, 1), (1, 1)))
    return padded[:, :, row_step:row_step + GR, 1 + col_step:1 + col_step + GC]

def deliver(terms, row_step, col_step):
    padded = jnp.pad(terms, ((0, 0), (0, 0), (1, 0), (1, 1)))
    return padded[:, :, 1 - row_step:1 - row_step + GR, 1 - col_step:1 - col_step + GC]

def validity(row_step, col_step):
    row_ids = jnp.arange(GR, dtype=jnp.int32)
    col_ids = jnp.arange(GC, dtype=jnp.int32)
    row_valid = row_ids + row_step < GR
    col_valid = (col_ids + col_step >= 0) & (col_ids + col_step < GC)
    return (row_valid[:, None] & col_valid[None, :]).astype(jnp.float32)

def link_state(affine, points_here, points_there, outlier_mask, direction):
    row_step, col_step = link_offsets[direction]
    weight_mask = outlier_mask[direction].astype(jnp.float32) * validity(row_step, col_step)[..., None]
    here = apply_affine(affine, points_here[direction])
    there = apply_affine(neighbour_of(affine, row_step, col_step), points_there[direction])
    return (weight_mask, here, there, link_error(here, there))

def reference(points_here, points_there, outlier_mask, transforms):
    affine = transforms
    records = []
    for iteration in range(ITERS):
        largest = jnp.zeros((), jnp.float32)
        total = jnp.zeros((), jnp.float32)
        count = jnp.zeros((), jnp.float32)
        for direction in range(4):
            weight_mask, here, there, error = link_state(affine, points_here, points_there, outlier_mask, direction)
            masked = weight_mask * error
            largest = jnp.maximum(largest, jnp.max(masked))
            total = total + jnp.sum(masked)
            count = count + jnp.sum(weight_mask)
        mean_error = total / jnp.maximum(count, 1.0)
        scale = 0.25 * largest + 1e-06
        damping = damping_scale * mean_error + 1.0
        gram = jnp.zeros((4, 4, GR, GC), jnp.float32)
        cross = jnp.zeros((3, 4, GR, GC), jnp.float32)
        for direction in range(4):
            row_step, col_step = link_offsets[direction]
            weight_mask, here, there, error = link_state(affine, points_here, points_there, outlier_mask, direction)
            weight = weight_mask / (1.0 + error / scale)
            gram = gram + gram_terms(weight, points_here[direction])
            cross = cross + cross_terms(weight, there, points_here[direction])
            gram = gram + deliver(gram_terms(weight, points_there[direction]), row_step, col_step)
            cross = cross + deliver(cross_terms(weight, here, points_there[direction]), row_step, col_step)
        identity = jnp.eye(4, dtype=jnp.float32)[:, :, None, None]
        affine = solve_small(gram + damping * identity, cross + damping * affine)
        records.append(jnp.stack([largest, mean_error]))
    return (affine, jnp.stack(records, axis=1))
```

```python
import jax
import jax.numpy as jnp
from jax import lax
from jax.experimental import pallas as pl
from jax.experimental.pallas import tpu as pltpu
from jax.sharding import PartitionSpec as P

ITERS = 2
MESH = pl.DeviceIdType.MESH
LINKS = ((0, 1), (1, 0), (1, 1), (1, -1))
ENDS = LINKS + tuple((-i, -j) for i, j in LINKS)
DAMPING = 64.0
LANES = 128
PAD = 8
F32 = jnp.float32


def pieces(step, size):
    inside = (max(0, -step), max(0, step), size - abs(step), 0)
    if step == 0:
        return [inside]
    if step > 0:
        return [inside, (size - step, 0, step, 1)]
    return [inside, (0, size + step, -step, -1)]


def solve(gram, cross):
    g = lambda a, b: gram[min(a, b), max(a, b)]
    low = [[None] * 4 for _ in range(4)]
    raw = [[None] * 4 for _ in range(4)]
    inv = [None] * 4
    for j in range(4):
        for i in range(j, 4):
            v = g(i, j)
            for k in range(j):
                v = v - low[i][k] * raw[j][k]
            raw[i][j] = v
        inv[j] = 1.0 / raw[j][j]
        for i in range(j + 1, 4):
            low[i][j] = raw[i][j] * inv[j]
    out = []
    for c in range(3):
        z = []
        for i in range(4):
            v = cross[c, i]
            for k in range(i):
                v = v - low[i][k] * z[k]
            z.append(v)
        s = [None] * 4
        for i in (3, 2, 1, 0):
            v = z[i] * inv[i]
            for k in range(i + 1, 4):
                v = v - low[k][i] * s[k]
            s[i] = v
        out.extend(s)
    return out


def make_kernel(n_row, n_col, rows, cols):
    halves = cols // 8
    wide = PAD + cols + 8
    last_r, last_c = PAD + cols - 1, PAD + cols

    remote = []
    local = []
    for d, (di, dj) in enumerate(LINKS):
        for sr, tr, nr, dr in pieces(di, rows):
            for sc, tc, nc, dc in pieces(dj, cols):
                entry = (d, pl.ds(sr, nr), pl.ds(sc, nc), pl.ds(tr, nr), pl.ds(tc, nc), dr, dc)
                (local if dr == 0 and dc == 0 else remote).append(entry)
    n_remote = 3 * len(remote)
    n_local = 3 * len(local)

    def kernel(
        here, there, mask, tf, aligned, stats,
        xs, zs, ms, wm, ys, errs, tfv, axl, edge, hrow, sums, msg, got_c, got_r, rec,
        own_sem, loc_sem, tf_sem, pts_send, pts_recv, halo_send, halo_recv,
        c_send, c_recv, r_send, r_recv,
    ):
        r = lax.axis_index("row")
        c = lax.axis_index("col")

        def at(dr, dc):
            return (lax.rem(r + dr + n_row, n_row), lax.rem(c + dc + n_col, n_col))

        barrier = pltpu.get_barrier_semaphore()
        for s in range(1, n_row):
            pl.semaphore_signal(barrier, inc=1, device_id=at(s, 0), device_id_type=MESH)
        for s in range(1, n_col):
            pl.semaphore_signal(barrier, inc=1, device_id=at(0, s), device_id_type=MESH)
        for dr in (-1, 1):
            for dc in (-1, 1):
                pl.semaphore_signal(barrier, inc=1, device_id=at(dr, dc), device_id_type=MESH)

        tf_copy = pltpu.make_async_copy(tf, tfv, tf_sem)
        tf_copy.start()
        own = [
            pltpu.make_async_copy(here, xs.at[pl.ds(0, 4)], own_sem.at[0]),
            pltpu.make_async_copy(there, zs.at[pl.ds(0, 4)], own_sem.at[1]),
            pltpu.make_async_copy(mask, ms.at[pl.ds(0, 4)], own_sem.at[2]),
        ]
        for copy in own:
            copy.start()
        inner = []
        for n, (d, sr, sc, tr, tc, _, _) in enumerate(local):
            inner += [
                pltpu.make_async_copy(
                    there.at[d, :, sr, sc, :], xs.at[4 + d, :, tr, tc, :], loc_sem.at[3 * n]),
                pltpu.make_async_copy(
                    here.at[d, :, sr, sc, :], zs.at[4 + d, :, tr, tc, :], loc_sem.at[3 * n + 1]),
                pltpu.make_async_copy(
                    mask.at[d, sr, sc, :], ms.at[4 + d, tr, tc, :], loc_sem.at[3 * n + 2]),
            ]
        for copy in inner:
            copy.start()

        lane = lax.broadcasted_iota(jnp.int32, (cols, LANES), 1)
        sub = lax.broadcasted_iota(jnp.int32, (cols, LANES), 0)
        eye = lane == sub
        row_lane = lax.broadcasted_iota(jnp.int32, (1, LANES), 1)

        def halo_copies(t):
            def send(n, src, dst, dr, dc):
                return pltpu.make_async_remote_copy(
                    src_ref=src, dst_ref=dst, send_sem=halo_send.at[t, n],
                    recv_sem=halo_recv.at[t, n], device_id=at(dr, dc), device_id_type=MESH)

            a = axl.at[t]
            every = pl.ds(0, 12)
            mid = pl.ds(1, rows)
            first, last = pl.ds(PAD, 1), pl.ds(last_r, 1)
            before, after = pl.ds(PAD - 1, 1), pl.ds(last_c, 1)
            top, bottom = pl.ds(1, 1), pl.ds(rows, 1)
            above, under = pl.ds(0, 1), pl.ds(rows + 1, 1)
            return [
                send(0, edge.at[t, 0], hrow.at[t, 1], -1, 0),
                send(1, edge.at[t, 1], hrow.at[t, 0], 1, 0),
                send(2, a.at[every, mid, first, :], a.at[every, mid, after, :], 0, -1),
                send(3, a.at[every, mid, last, :], a.at[every, mid, before, :], 0, 1),
                send(4, a.at[every, top, first, :], a.at[every, under, after, :], -1, -1),
                send(5, a.at[every, top, last, :], a.at[every, under, before, :], -1, 1),
                send(6, a.at[every, bottom, first, :], a.at[every, above, after, :], 1, -1),
                send(7, a.at[every, bottom, last, :], a.at[every, above, before, :], 1, 1),
            ]

        def publish(t):
            for side, i in ((0, 0), (1, rows - 1)):
                packed = jnp.zeros((cols, LANES), F32)
                for k in range(12):
                    packed = jnp.where(lane == k, axl[t, k, 1 + i, PAD : PAD + cols, :], packed)
                edge[t, side] = packed

        tf_copy.wait()
        for k in range(12):
            for i in range(rows):
                line = tfv[k // 4, k % 4, i : i + 1, :]
                spread = jnp.where(eye[:, :cols], jnp.broadcast_to(line, (cols, cols)), 0.0)
                value = jnp.sum(spread, axis=1, keepdims=True)
                axl[0, k, 1 + i, PAD : PAD + cols, :] = jnp.broadcast_to(value, (cols, LANES))
        publish(0)

        pl.semaphore_wait(barrier, n_row - 1 + n_col - 1 + 4)

        halos = halo_copies(0)
        for copy in halos:
            copy.start()
        outer = []
        for n, (d, sr, sc, tr, tc, dr, dc) in enumerate(remote):
            for m, (src, dst) in enumerate((
                (there.at[d, :, sr, sc, :], xs.at[4 + d, :, tr, tc, :]),
                (here.at[d, :, sr, sc, :], zs.at[4 + d, :, tr, tc, :]),
                (mask.at[d, sr, sc, :], ms.at[4 + d, tr, tc, :]),
            )):
                outer.append(pltpu.make_async_remote_copy(
                    src_ref=src, dst_ref=dst, send_sem=pts_send.at[3 * n + m],
                    recv_sem=pts_recv.at[3 * n + m], device_id=at(dr, dc),
                    device_id_type=MESH))
        for copy in outer:
            copy.start()

        def masks(e):
            di, dj = ENDS[e]
            j = c * cols + sub + dj
            keep_col = (j >= 0) & (j < n_col * cols)
            for i in range(rows):
                row = r * rows + i + di
                keep = keep_col & (row >= 0) & (row < n_row * rows)
                wm[e, i] = jnp.where(keep, ms[e, i].astype(F32), 0.0)

        for copy in own:
            copy.wait()
        for e in range(4):
            masks(e)
        count = jnp.zeros((8, LANES), F32)
        for e in range(4):
            for i in range(rows):
                for h in range(halves):
                    count = count + wm[e, i, 8 * h : 8 * h + 8, :]

        def all_sum(x):
            return jnp.sum(jnp.sum(x, axis=0, keepdims=True), axis=1, keepdims=True)

        def all_max(x):
            return jnp.max(jnp.max(x, axis=0, keepdims=True), axis=1, keepdims=True)

        count = all_sum(count)

        def errors(t, group, carry):
            def body(i, carry):
                top, total = carry
                for h in range(halves):
                    lo = 8 * h
                    own_map = [axl[t, k, 1 + i, PAD + lo : PAD + lo + 8, :] for k in range(12)]
                    for e in group:
                        di, dj = ENDS[e]
                        x = [xs[e, n, i, lo : lo + 8, :] for n in range(3)]
                        z = [zs[e, n, i, lo : lo + 8, :] for n in range(3)]
                        err = None
                        for q in range(3):
                            far = [
                                axl[t, 4 * q + k, 1 + di + i,
                                    PAD + dj + lo : PAD + dj + lo + 8, :]
                                for k in range(4)
                            ]
                            y = far[3] + far[0] * z[0]
                            y = y + far[1] * z[1]
                            y = y + far[2] * z[2]
                            ys[e, q, i, lo : lo + 8, :] = y
                            a = own_map[4 * q + 3] + own_map[4 * q] * x[0]
                            a = a + own_map[4 * q + 1] * x[1]
                            a = a + own_map[4 * q + 2] * x[2]
                            gap = a - y
                            err = gap * gap if err is None else err + gap * gap
                        errs[e, i, lo : lo + 8, :] = err
                        if carry is not None:
                            masked = wm[e, i, lo : lo + 8, :] * err
                            top = jnp.maximum(top, masked)
                            total = total + masked
                return top, total

            return lax.fori_loop(0, rows, body, carry)

        def moments(scale):
            def body(i, _):
                for h in range(halves):
                    lo = 8 * h
                    acc = [None] * 22
                    for e in range(8):
                        w = wm[e, i, lo : lo + 8, :] * (scale / (scale + errs[e, i, lo : lo + 8, :]))
                        x = [xs[e, n, i, lo : lo + 8, :] for n in range(3)]
                        y = [ys[e, n, i, lo : lo + 8, :] for n in range(3)]
                        wx = [w * v for v in x]
                        new = []
                        for a in range(3):
                            for b in range(a, 3):
                                new.append(wx[a] * x[b])
                            new.append(wx[a])
                        new.append(w)
                        for q in range(3):
                            wy = w * y[q]
                            new += [wy * v for v in x]
                            new.append(wy)
                        acc = [n if a is None else a + n for a, n in zip(acc, new)]
                    for n in range(22):
                        total = jnp.sum(acc[n], axis=1, keepdims=True)
                        sums[n, i, lo : lo + 8, :] = jnp.broadcast_to(total, (8, LANES))
                return 0

            lax.fori_loop(0, rows, body, 0)

        pending = []
        for t in range(ITERS):
            for n in (0, 2, 3, 4, 5, 1, 6, 7):
                halos[n].wait_recv()
            for side, row in ((1, rows + 1), (0, 0)):
                block = hrow[t, side]
                for k in range(12):
                    axl[t, k, row, PAD : PAD + cols, :] = jnp.broadcast_to(
                        block[:, k : k + 1], (cols, LANES))
            zero = jnp.zeros((8, LANES), F32)
            top, total = errors(t, range(4), (zero, zero))
            top, total = all_max(top), all_sum(total)
            packed = jnp.where(row_lane < 32, top, jnp.where(row_lane < 64, total, count))

            def combine(block):
                return jnp.where(
                    row_lane < 32, jnp.max(block, axis=0, keepdims=True),
                    jnp.sum(block, axis=0, keepdims=True))

            def share(packed, stage, got, me, size, send_sem, recv_sem, target):
                msg[t, stage] = packed
                got[t, pl.ds(me, 1), :] = packed
                for s in range(1, size):
                    pltpu.make_async_remote_copy(
                        src_ref=msg.at[t, stage], dst_ref=got.at[t, pl.ds(me, 1), :],
                        send_sem=send_sem.at[t], recv_sem=recv_sem.at[t],
                        device_id=target(s), device_id_type=MESH).start()

            def arrived(got, size, sem):
                block = got.at[t, pl.ds(0, size - 1), :]
                pltpu.make_async_copy(block, block, sem.at[t]).wait()

            share(packed, 0, got_c, c, n_col, c_send, c_recv, lambda s: at(0, s))
            arrived(got_c, n_col, c_recv)
            share(combine(got_c[t]), 1, got_r, r, n_row, r_send, r_recv, lambda s: at(s, 0))
            if t == 0:
                for copy in inner:
                    copy.wait()
                for copy in outer:
                    copy.wait_recv()
                for e in range(4, 8):
                    masks(e)
            errors(t, range(4, 8), (zero, zero))
            arrived(got_r, n_row, r_recv)
            packed = combine(got_r[t])
            largest, total, number = packed[:, 0:1], packed[:, 32:33], packed[:, 64:65]
            mean = total / jnp.maximum(number, 1.0)
            scale = 0.25 * largest + 1e-6
            damping = DAMPING * mean + 1.0
            rec[t, 0] = jnp.broadcast_to(largest, (1, LANES))
            rec[t, 1] = jnp.broadcast_to(mean, (1, LANES))
            moments(jnp.broadcast_to(scale, (8, LANES)))
            damp = jnp.broadcast_to(damping, (cols, LANES))
            for i in range(rows):
                old = [axl[t, k, 1 + i, PAD : PAD + cols, :] for k in range(12)]
                gram, n = {}, 0
                for a in range(4):
                    for b in range(a, 4):
                        gram[a, b] = sums[n, i] + damp if a == b else sums[n, i]
                        n += 1
                cross = {}
                for q in range(3):
                    for b in range(4):
                        cross[q, b] = sums[n, i] + damp * old[4 * q + b]
                        n += 1
                new = solve(gram, cross)
                if t + 1 < ITERS:
                    for k in range(12):
                        axl[t + 1, k, 1 + i, PAD : PAD + cols, :] = new[k]
                else:
                    for k in range(12):
                        line = jnp.sum(jnp.where(eye, new[k], 0.0), axis=0, keepdims=True)
                        aligned[k // 4, k % 4, i : i + 1, :] = line[:, :cols]
            pending += halos
            if t + 1 < ITERS:
                publish(t + 1)
                halos = halo_copies(t + 1)
                for copy in halos:
                    copy.start()

        a = lax.broadcasted_iota(jnp.int32, (2, 2), 1)
        b = lax.broadcasted_iota(jnp.int32, (2, 2), 0)
        stats[...] = jnp.where(
            b == 0,
            jnp.where(a == 0, rec[0, 0][:, :2], rec[1, 0][:, :2]),
            jnp.where(a == 0, rec[0, 1][:, :2], rec[1, 1][:, :2]))

        for copy in pending + outer:
            copy.wait_send()
        for t in range(ITERS):
            for got, size, sem in ((got_c, n_col, c_send), (got_r, n_row, r_send)):
                block = got.at[t, pl.ds(0, size - 1), :]
                pltpu.make_async_copy(block, block, sem.at[t]).wait()

    dma = pltpu.SemaphoreType.DMA
    vm = pltpu.VMEM
    scratch = [
        vm((8, 3, rows, cols, LANES), F32),
        vm((8, 3, rows, cols, LANES), F32),
        vm((8, rows, cols, LANES), jnp.int32),
        vm((8, rows, cols, LANES), F32),
        vm((8, 3, rows, cols, LANES), F32),
        vm((8, rows, cols, LANES), F32),
        vm((3, 4, rows, cols), F32),
        vm((ITERS, 12, rows + 2, wide, LANES), F32),
        vm((ITERS, 2, cols, LANES), F32),
        vm((ITERS, 2, cols, LANES), F32),
        vm((22, rows, cols, LANES), F32),
        vm((ITERS, 2, 1, LANES), F32),
        vm((ITERS, n_col, LANES), F32),
        vm((ITERS, n_row, LANES), F32),
        vm((ITERS, 2, 1, LANES), F32),
        dma((3,)), dma((n_local,)), dma(()),
        dma((n_remote,)), dma((n_remote,)),
        dma((ITERS, 8)), dma((ITERS, 8)),
        dma((ITERS,)), dma((ITERS,)), dma((ITERS,)), dma((ITERS,)),
    ]
    return kernel, scratch


def solution(mesh):
    n_row, n_col = mesh.shape["row"], mesh.shape["col"]

    def on_device(points_here, points_there, outlier_mask, transforms):
        rows, cols = transforms.shape[2:]
        kernel, scratch = make_kernel(n_row, n_col, rows, cols)
        hbm = pl.BlockSpec(memory_space=pl.ANY)
        return pl.pallas_call(
            kernel,
            out_shape=(
                jax.ShapeDtypeStruct(transforms.shape, F32),
                jax.ShapeDtypeStruct((2, ITERS), F32),
            ),
            in_specs=[hbm] * 4,
            out_specs=(pl.BlockSpec(memory_space=pltpu.VMEM),) * 2,
            scratch_shapes=scratch,
            compiler_params=pltpu.CompilerParams(
                collective_id=0, has_side_effects=True, vmem_limit_bytes=48 << 20),
        )(points_here, points_there, outlier_mask, transforms)

    placed = (
        P(None, None, "row", "col", None),
        P(None, None, "row", "col", None),
        P(None, "row", "col", None),
        P(None, None, "row", "col"),
    )
    return jax.shard_map(
        on_device, mesh=mesh, in_specs=placed,
        out_specs=(P(None, None, "row", "col"), P()), check_vma=False)
```

```python
import jax
import jax.numpy as jnp
from jax import lax
from jax.experimental import pallas as pl
from jax.experimental.pallas import tpu as pltpu
from jax.sharding import PartitionSpec as P

ITERS = 2
MESH = pl.DeviceIdType.MESH
LINKS = ((0, 1), (1, 0), (1, 1), (1, -1))
DAMPING = 64.0
LANES = 128
RING = 2
WIDE = 32
COL0 = 3
NX, NY = 4, 8
F32 = jnp.float32


def solve(gram, cross):
    g = lambda a, b: gram[min(a, b), max(a, b)]
    low = [[None] * 4 for _ in range(4)]
    raw = [[None] * 4 for _ in range(4)]
    inv = [None] * 4
    for j in range(4):
        for i in range(j, 4):
            v = g(i, j)
            for k in range(j):
                v = v - low[i][k] * raw[j][k]
            raw[i][j] = v
        inv[j] = 1.0 / raw[j][j]
        for i in range(j + 1, 4):
            low[i][j] = raw[i][j] * inv[j]
    out = []
    for c in range(3):
        z = []
        for i in range(4):
            v = cross[c, i]
            for k in range(i):
                v = v - low[i][k] * z[k]
            z.append(v)
        s = [None] * 4
        for i in (3, 2, 1, 0):
            v = z[i] * inv[i]
            for k in range(i + 1, 4):
                v = v - low[k][i] * s[k]
            s[i] = v
        out.extend(s)
    return out


def make_kernel(n_row, n_col, rows, cols):
    around = [(a, b) for a in (-1, 0, 1) for b in (-1, 0, 1) if (a, b) != (0, 0)]
    span = rows + 2 * RING - 1

    def kernel(
        here, there, mask, tf, aligned, stats,
        xs, zs, ms, wm, wt, hm, tm, errs, tfv, axl, sums, msg, got_c, got_r, rec,
        own_sem, tf_sem, pts_send, pts_recv, tf_send, tf_recv,
        c_send, c_recv, r_send, r_recv, known,
    ):
        r = lax.axis_index("row")
        c = lax.axis_index("col")
        x0, y0 = r // NY, lax.rem(r, NY)
        up, down, left, right = r > 0, r < n_row - 1, c > 0, c < n_col - 1
        side = {(-1, 0): up, (1, 0): down, (0, -1): left, (0, 1): right}

        def exists(dr, dc):
            if dr and dc:
                return side[dr, 0] & side[0, dc]
            return side[dr, dc]

        def at_col(s):
            return (r, lax.rem(c + s + n_col, n_col))

        def at_xy(dx, dy):
            return (lax.rem(x0 + dx + NX, NX) * NY + lax.rem(y0 + dy + NY, NY), c)

        def signal(sem, device):
            pl.semaphore_signal(sem, inc=1, device_id=device, device_id_type=MESH)

        one = lambda flag: flag.astype(jnp.int32)
        barrier = pltpu.get_barrier_semaphore()
        steps_xy = ((0, 1), (0, -1), (1, 0), (-1, 0))
        for d in steps_xy:
            signal(barrier, at_xy(*d))
        for s in (1, -1, 2, -2):
            signal(barrier, at_col(s))
        greeted = 8
        cross_up, cross_down = up & (y0 == 0), down & (y0 == NY - 1)
        for dr, dc, flag in (
            (-1, 0, cross_up), (1, 0, cross_down),
            (-1, -1, exists(-1, -1)), (-1, 1, exists(-1, 1)),
            (1, -1, exists(1, -1)), (1, 1, exists(1, 1)),
        ):
            greeted = greeted + one(flag)

            @pl.when(flag)
            def _():
                signal(barrier, (r + dr, c + dc))

        middle_r, middle_c = pl.ds(RING, rows), pl.ds(COL0, cols)
        own = [
            pltpu.make_async_copy(tf, tfv.at[4], tf_sem),
            pltpu.make_async_copy(mask, ms.at[:, middle_r, middle_c, :], own_sem.at[2]),
            pltpu.make_async_copy(here, xs.at[:, :, middle_r, middle_c, :], own_sem.at[0]),
            pltpu.make_async_copy(there, zs.at[:, :, middle_r, middle_c, :], own_sem.at[1]),
        ]
        for copy in own:
            copy.start()

        for dr, dc in around:
            @pl.when(jnp.logical_not(exists(dr, dc)))
            def _():
                tfv[(dr + 1) * 3 + dc + 1] = jnp.zeros((3, 4, rows, cols), F32)

        def blank(row_part, col_part):
            for buf in (xs, zs):
                shape = (4, 3, row_part.size, col_part.size, LANES)
                buf[:, :, row_part, col_part, :] = jnp.zeros(shape, F32)

        for flag, row_part, col_part in (
            (up, pl.ds(0, RING), pl.ds(0, WIDE)),
            (down, pl.ds(RING + rows, 1), pl.ds(0, WIDE)),
            (left, pl.ds(0, span), pl.ds(0, COL0)),
            (right, pl.ds(0, span), pl.ds(COL0 + cols, RING)),
        ):
            @pl.when(jnp.logical_not(flag))
            def _():
                blank(row_part, col_part)

        lane16 = lax.broadcasted_iota(jnp.int32, (8, cols), 1)
        sub8 = lax.broadcasted_iota(jnp.int32, (8, cols), 0)
        row_lane = lax.broadcasted_iota(jnp.int32, (1, LANES), 1)

        pl.semaphore_wait(barrier, greeted)

        def tf_copy(n, dr, dc):
            return pltpu.make_async_remote_copy(
                src_ref=tf, dst_ref=tfv.at[(1 - dr) * 3 + 1 - dc], send_sem=tf_send.at[n],
                recv_sem=tf_recv.at[n], device_id=(r + dr, c + dc), device_id_type=MESH)

        def tf_arrived(dr, dc):
            n = around.index((-dr, -dc))

            @pl.when(exists(dr, dc))
            def _():
                tf_copy(n, -dr, -dc).wait_recv()

        for dr, dc in ((1, 1), (1, -1), (-1, 1), (-1, -1), (1, 0), (-1, 0), (0, 1), (0, -1)):
            @pl.when(exists(dr, dc))
            def _():
                tf_copy(around.index((dr, dc)), dr, dc).start()

        for d in steps_xy:
            signal(known.at[0], at_xy(*d))
        signal(known.at[0], at_col(2))
        signal(known.at[0], at_col(-2))

        part_r = {1: (rows - RING, 0, RING), 0: (0, RING, rows), -1: (0, RING + rows, 1)}
        part_c = {
            1: (cols - RING, COL0 - RING, RING), 0: (0, COL0, cols), -1: (0, COL0 + cols, RING)}

        def outer(dr, dc):
            n = around.index((dr, dc))
            sr, tr, nr = part_r[dr]
            sc, tc, nc = part_c[dc]
            src = (pl.ds(sr, nr), pl.ds(sc, nc), slice(None))
            dst = (pl.ds(tr, nr), pl.ds(tc, nc), slice(None))
            every = (slice(None),)
            return [
                pltpu.make_async_remote_copy(
                    src_ref=a.at[lead + src], dst_ref=b.at[lead + dst],
                    send_sem=pts_send.at[n, m], recv_sem=pts_recv.at[n, m],
                    device_id=(r + dr, c + dc), device_id_type=MESH)
                for m, (a, b, lead) in enumerate(
                    ((here, xs, every * 2), (there, zs, every * 2), (mask, ms, every)))
            ]

        for dr, dc in around:
            @pl.when(exists(dr, dc))
            def _():
                for copy in outer(dr, dc):
                    copy.start()

        def masks(d, i, lo, size):
            di, dj = LINKS[d]
            sub = lax.broadcasted_iota(jnp.int32, (size, LANES), 0)
            j = c * cols + sub + (lo - COL0)
            k = j + dj
            row = r * rows + i
            keep_row = (row >= 0) & (row + di < n_row * rows)
            keep = (j >= 0) & (j < n_col * cols) & (k >= 0) & (k < n_col * cols) & keep_row
            wm[d, RING + i, lo : lo + size, :] = jnp.where(
                keep, ms[d, RING + i, lo : lo + size, :].astype(F32), 0.0)

        own[1].wait()
        count = jnp.zeros((cols, LANES), F32)
        for d in range(4):
            for i in range(rows):
                masks(d, i, COL0, cols)
                count = count + wm[d, RING + i, COL0 : COL0 + cols, :]

        def all_sum(x):
            return jnp.sum(jnp.sum(x, axis=0, keepdims=True), axis=1, keepdims=True)

        def all_max(x):
            return jnp.max(jnp.max(x, axis=0, keepdims=True), axis=1, keepdims=True)

        count = all_sum(count)

        pl.semaphore_wait(known.at[0], 6)
        for device in (at_xy(0, 2), at_xy(0, -2), at_xy(2, 0), at_col(4), at_col(-4)):
            signal(known.at[1], device)

        own_lane = lane16 - sub8
        picks = (
            ((4, own_lane == -COL0), (3, own_lane == cols - COL0)),
            ((4, own_lane == 8 - COL0),),
            ((4, own_lane == 16 - COL0), (5, own_lane == 16 - COL0 - cols)),
        )

        def expand(i):
            base = 3 if 0 <= i < rows else (0 if i < 0 else 6)
            row = i % rows
            for k in range(12):
                for b, pick in enumerate(picks):
                    total = None
                    for slot, chosen in pick:
                        line = tfv[base + slot - 3, k // 4, k % 4, row : row + 1, :]
                        part = jnp.where(chosen, jnp.broadcast_to(line, (8, cols)), 0.0)
                        total = part if total is None else total + part
                    value = jnp.sum(total, axis=1, keepdims=True)
                    axl[0, k, RING + i, 8 * b : 8 * b + 8, :] = jnp.broadcast_to(value, (8, LANES))

        def errors(t, first, last, starts, carry=None):
            def body(i, carry):
                for lo in starts:
                    own_map = [axl[t, k, i, lo : lo + 8, :] for k in range(12)]
                    for d in range(4):
                        di, dj = LINKS[d]
                        x = [xs[d, n, i, lo : lo + 8, :] for n in range(3)]
                        z = [zs[d, n, i, lo : lo + 8, :] for n in range(3)]
                        err = None
                        for q in range(3):
                            far = [
                                axl[t, 4 * q + k, i + di, lo + dj : lo + dj + 8, :]
                                for k in range(4)
                            ]
                            y = far[3] + far[0] * z[0]
                            y = y + far[1] * z[1]
                            y = y + far[2] * z[2]
                            tm[d, q, i, lo : lo + 8, :] = y
                            a = own_map[4 * q + 3] + own_map[4 * q] * x[0]
                            a = a + own_map[4 * q + 1] * x[1]
                            a = a + own_map[4 * q + 2] * x[2]
                            hm[d, q, i, lo : lo + 8, :] = a
                            gap = a - y
                            err = gap * gap if err is None else err + gap * gap
                        errs[d, i, lo : lo + 8, :] = err
                        if carry is not None:
                            masked = wm[d, i, lo : lo + 8, :] * err
                            carry = (jnp.maximum(carry[0], masked), carry[1] + masked)
                return carry

            if carry is None:
                lax.fori_loop(first, last, lambda i, _: body(i, None) or 0, 0)
                return None
            return lax.fori_loop(first, last, body, carry)

        def weights(first, last, starts, scale):
            def body(i, _):
                for lo in starts:
                    for d in range(4):
                        at = (d, i, slice(lo, lo + 8))
                        wt[at] = wm[at] * (scale / (scale + errs[at]))
                return 0

            lax.fori_loop(first, last, body, 0)

        def moments(first, last, starts):
            def body(i, _):
                for lo in starts:
                    acc = [None] * 22
                    for e in range(8):
                        d = e % 4
                        di, dj = LINKS[d] if e >= 4 else (0, 0)
                        p, q = i - di, lo - dj
                        w = wt[d, p, q : q + 8, :]
                        mine, other = (xs, tm) if e < 4 else (zs, hm)
                        x = [mine[d, n, p, q : q + 8, :] for n in range(3)]
                        y = [other[d, n, p, q : q + 8, :] for n in range(3)]
                        wx = [w * v for v in x]
                        new = []
                        for a in range(3):
                            for b in range(a, 3):
                                new.append(wx[a] * x[b])
                            new.append(wx[a])
                        new.append(w)
                        for n in range(3):
                            wy = w * y[n]
                            new += [wy * v for v in x]
                            new.append(wy)
                        acc = [n if a is None else a + n for a, n in zip(acc, new)]
                    for n in range(22):
                        total = jnp.sum(acc[n], axis=1, keepdims=True)
                        sums[n, i, lo : lo + 8, :] = jnp.broadcast_to(total, (8, LANES))
                return 0

            lax.fori_loop(first, last, body, 0)

        own[0].wait()
        for spot in ((0, 1), (0, -1), (1, 0), (1, 1), (1, -1)):
            tf_arrived(*spot)
        for i in range(rows + 1):
            expand(i)
        own[2].wait()
        own[3].wait()

        def combine(block):
            return jnp.where(
                row_lane < 32, jnp.max(block, axis=0, keepdims=True),
                jnp.sum(block, axis=0, keepdims=True))

        def share(t, packed, stage, got, me, send_sem, recv_sem, targets):
            msg[t, stage] = packed
            got[t, pl.ds(me, 1), :] = packed
            for device in targets:
                pltpu.make_async_remote_copy(
                    src_ref=msg.at[t, stage], dst_ref=got.at[t, pl.ds(me, 1), :],
                    send_sem=send_sem.at[t], recv_sem=recv_sem.at[t],
                    device_id=device, device_id_type=MESH).start()

        def arrived(t, got, size, sem):
            block = got.at[t, pl.ds(0, size - 1), :]
            pltpu.make_async_copy(block, block, sem.at[t]).wait()

        col_targets = [at_col(s) for s in sorted(range(1, n_col), key=lambda s: -min(s, n_col - s))]
        plane = [(a, b) for a in range(NX) for b in range(NY) if a or b]
        plane.sort(key=lambda p: -(min(p[0], NX - p[0]) + min(p[1], NY - p[1])))
        row_targets = [at_xy(*p) for p in plane]

        own_starts = tuple(range(COL0, COL0 + cols, 8))
        for t in range(ITERS):
            zero = jnp.zeros((8, LANES), F32)
            top, total = errors(t, RING, RING + rows, own_starts, (zero, zero))
            top, total = all_max(top), all_sum(total)
            packed = jnp.where(row_lane < 32, top, jnp.where(row_lane < 64, total, count))
            if t == 0:
                pl.semaphore_wait(known.at[1], 5)
                signal(known.at[2], at_xy(0, 4))
            share(t, packed, 0, got_c, c, c_send, c_recv, col_targets)
            if t == 0:
                for spot in ((-1, 0), (-1, -1), (-1, 1)):
                    tf_arrived(*spot)
                for i in (-2, -1, rows + 1):
                    expand(i)
                pl.semaphore_wait(known.at[2], 1)
            else:
                errors(t, RING - 1, RING, (2, 10, 18))
                errors(t, RING, RING + rows, (2, 18))
            arrived(t, got_c, n_col, c_recv)
            share(t, combine(got_c[t]), 1, got_r, r, r_send, r_recv, row_targets)
            if t == 0:
                for dr, dc in around:
                    @pl.when(exists(dr, dc))
                    def _():
                        for copy in outer(-dr, -dc):
                            copy.wait_recv()
                for d in range(4):
                    for i in range(-RING, rows + 1):
                        if 0 <= i < rows:
                            masks(d, i, 0, 8)
                            masks(d, i, 16, 8)
                        else:
                            masks(d, i, 0, 24)
                errors(t, 0, RING, (1, 9, 17))
                errors(t, RING + rows, RING + rows + 1, (1, 9, 17))
                errors(t, RING, RING + rows, (1, 17))
            arrived(t, got_r, n_row, r_recv)
            packed = combine(got_r[t])
            largest, total, number = packed[:, 0:1], packed[:, 32:33], packed[:, 64:65]
            mean = total / jnp.maximum(number, 1.0)
            scale = jnp.broadcast_to(0.25 * largest + 1e-6, (8, LANES))
            damping = DAMPING * mean + 1.0
            rec[t, 0] = jnp.broadcast_to(largest, (1, LANES))
            rec[t, 1] = jnp.broadcast_to(mean, (1, LANES))
            if t == 0:
                weights(0, span, (1, 9, 17), scale)
                first, last, lo, size = RING - 1, RING + rows + 1, COL0 - 1, 24
            else:
                weights(RING - 1, RING + rows, (2, 10, 18), scale)
                first, last, lo, size = RING, RING + rows, COL0, cols
            moments(first, last, range(lo, lo + size, 8))
            damp = jnp.broadcast_to(damping, (size, LANES))
            for i in range(first, last):
                old = [axl[t, k, i, lo : lo + size, :] for k in range(12)]
                gram, n = {}, 0
                for a in range(4):
                    for b in range(a, 4):
                        part = sums[n, i, lo : lo + size, :]
                        gram[a, b] = part + damp if a == b else part
                        n += 1
                cross = {}
                for q in range(3):
                    for b in range(4):
                        cross[q, b] = sums[n, i, lo : lo + size, :] + damp * old[4 * q + b]
                        n += 1
                new = solve(gram, cross)
                if t + 1 < ITERS:
                    for k in range(12):
                        axl[t + 1, k, i, lo : lo + size, :] = new[k]
                else:
                    lane = lax.broadcasted_iota(jnp.int32, (size, LANES), 1)
                    sub = lax.broadcasted_iota(jnp.int32, (size, LANES), 0)
                    for k in range(12):
                        line = jnp.sum(jnp.where(lane == sub, new[k], 0.0), axis=0, keepdims=True)
                        aligned[k // 4, k % 4, i - first : i - first + 1, :] = line[:, :cols]

        a = lax.broadcasted_iota(jnp.int32, (2, 2), 1)
        b = lax.broadcasted_iota(jnp.int32, (2, 2), 0)
        stats[...] = jnp.where(
            b == 0,
            jnp.where(a == 0, rec[0, 0][:, :2], rec[1, 0][:, :2]),
            jnp.where(a == 0, rec[0, 1][:, :2], rec[1, 1][:, :2]))

        for dr, dc in around:
            @pl.when(exists(dr, dc))
            def _():
                tf_copy(around.index((dr, dc)), dr, dc).wait_send()
                for copy in outer(dr, dc):
                    copy.wait_send()
        for t in range(ITERS):
            arrived(t, got_c, n_col, c_send)
            arrived(t, got_r, n_row, r_send)

    dma = pltpu.SemaphoreType.DMA
    vm = pltpu.VMEM
    grid = (span, WIDE, LANES)
    scratch = [
        vm((4, 3) + grid, F32),
        vm((4, 3) + grid, F32),
        vm((4,) + grid, jnp.int32),
        vm((4,) + grid, F32),
        vm((4,) + grid, F32),
        vm((4, 3) + grid, F32),
        vm((4, 3) + grid, F32),
        vm((4,) + grid, F32),
        vm((9, 3, 4, rows, cols), F32),
        vm((ITERS, 12, rows + 2 * RING, WIDE, LANES), F32),
        vm((22,) + grid, F32),
        vm((ITERS, 2, 1, LANES), F32),
        vm((ITERS, n_col, LANES), F32),
        vm((ITERS, n_row, LANES), F32),
        vm((ITERS, 2, 1, LANES), F32),
        dma((3,)), dma(()),
        dma((8, 3)), dma((8, 3)),
        dma((8,)), dma((8,)),
        dma((ITERS,)), dma((ITERS,)), dma((ITERS,)), dma((ITERS,)),
        pltpu.SemaphoreType.REGULAR((3,)),
    ]
    return kernel, scratch


def solution(mesh):
    n_row, n_col = mesh.shape["row"], mesh.shape["col"]

    def on_device(points_here, points_there, outlier_mask, transforms):
        rows, cols = transforms.shape[2:]
        kernel, scratch = make_kernel(n_row, n_col, rows, cols)
        hbm = pl.BlockSpec(memory_space=pltpu.HBM)
        return pl.pallas_call(
            kernel,
            out_shape=(
                jax.ShapeDtypeStruct(transforms.shape, F32),
                jax.ShapeDtypeStruct((2, ITERS), F32),
            ),
            in_specs=[hbm] * 4,
            out_specs=(pl.BlockSpec(memory_space=pltpu.VMEM),) * 2,
            scratch_shapes=scratch,
            compiler_params=pltpu.CompilerParams(collective_id=0, has_side_effects=True),
        )(points_here, points_there, outlier_mask, transforms)

    placed = (
        P(None, None, "row", "col", None),
        P(None, None, "row", "col", None),
        P(None, "row", "col", None),
        P(None, None, "row", "col"),
    )
    return jax.shard_map(
        on_device, mesh=mesh, in_specs=placed,
        out_specs=(P(None, None, "row", "col"), P()), check_vma=False)
```

```python
import jax
import jax.numpy as jnp
from jax import lax
from jax.experimental import pallas as pl
from jax.experimental.pallas import tpu as pltpu
from jax.sharding import PartitionSpec as P

ITERS = 2
MESH = pl.DeviceIdType.MESH
LINKS = ((0, 1), (1, 0), (1, 1), (1, -1))
DAMPING = 64.0
LANES = 128
RING = 2
WIDE = 32
COL0 = 3
NX, NY = 4, 8
F32 = jnp.float32


def solve(gram, cross):
    g = lambda a, b: gram[min(a, b), max(a, b)]
    low = [[None] * 4 for _ in range(4)]
    raw = [[None] * 4 for _ in range(4)]
    inv = [None] * 4
    for j in range(4):
        for i in range(j, 4):
            v = g(i, j)
            for k in range(j):
                v = v - low[i][k] * raw[j][k]
            raw[i][j] = v
        inv[j] = 1.0 / raw[j][j]
        for i in range(j + 1, 4):
            low[i][j] = raw[i][j] * inv[j]
    out = []
    for c in range(3):
        z = []
        for i in range(4):
            v = cross[c, i]
            for k in range(i):
                v = v - low[i][k] * z[k]
            z.append(v)
        s = [None] * 4
        for i in (3, 2, 1, 0):
            v = z[i] * inv[i]
            for k in range(i + 1, 4):
                v = v - low[k][i] * s[k]
            s[i] = v
        out.extend(s)
    return out


def make_kernel(n_row, n_col, rows, cols):
    around = [(a, b) for a in (-1, 0, 1) for b in (-1, 0, 1) if (a, b) != (0, 0)]
    span = rows + 2 * RING - 1

    def kernel(
        here, there, mask, tf, aligned, stats,
        xs, zs, ms, wm, wt, hm, tm, errs, tfv, axl, sums, msg, got_c, got_r, rec,
        own_sem, tf_sem, pts_send, pts_recv, tf_send, tf_recv,
        c_send, c_recv, r_send, r_recv, edge_send, edge_recv, known,
    ):
        r = lax.axis_index("row")
        c = lax.axis_index("col")
        x0, y0 = r // NY, lax.rem(r, NY)
        up, down, left, right = r > 0, r < n_row - 1, c > 0, c < n_col - 1
        side = {(-1, 0): up, (1, 0): down, (0, -1): left, (0, 1): right}

        def exists(dr, dc):
            if dr and dc:
                return side[dr, 0] & side[0, dc]
            return side[dr, dc]

        def at_col(s):
            return (r, lax.rem(c + s + n_col, n_col))

        def at_xy(dx, dy):
            return (lax.rem(x0 + dx + NX, NX) * NY + lax.rem(y0 + dy + NY, NY), c)

        def signal(sem, device):
            pl.semaphore_signal(sem, inc=1, device_id=device, device_id_type=MESH)

        one = lambda flag: flag.astype(jnp.int32)
        barrier = pltpu.get_barrier_semaphore()
        steps_xy = ((0, 1), (0, -1), (1, 0), (-1, 0))
        for d in steps_xy:
            signal(barrier, at_xy(*d))
        for s in (1, -1, 2, -2):
            signal(barrier, at_col(s))
        greeted = 8
        cross_up, cross_down = up & (y0 == 0), down & (y0 == NY - 1)
        for dr, dc, flag in (
            (-1, 0, cross_up), (1, 0, cross_down),
            (-1, -1, exists(-1, -1)), (-1, 1, exists(-1, 1)),
            (1, -1, exists(1, -1)), (1, 1, exists(1, 1)),
        ):
            greeted = greeted + one(flag)

            @pl.when(flag)
            def _():
                signal(barrier, (r + dr, c + dc))

        middle_r, middle_c = pl.ds(RING, rows), pl.ds(COL0, cols)
        own = [
            pltpu.make_async_copy(tf, tfv.at[4], tf_sem),
            pltpu.make_async_copy(mask, ms.at[:, middle_r, middle_c, :], own_sem.at[2]),
            pltpu.make_async_copy(here, xs.at[:, :, middle_r, middle_c, :], own_sem.at[0]),
            pltpu.make_async_copy(there, zs.at[:, :, middle_r, middle_c, :], own_sem.at[1]),
        ]
        for copy in own:
            copy.start()

        edges = (
            (1, 0, pl.ds(RING + rows - 1, 1), pl.ds(COL0, cols), pl.ds(RING - 1, 1), pl.ds(COL0, cols)),
            (1, 1, pl.ds(RING + rows - 1, 1), pl.ds(COL0 + cols - 1, 1),
             pl.ds(RING - 1, 1), pl.ds(COL0 - 1, 1)),
            (1, -1, pl.ds(RING + rows - 1, 1), pl.ds(COL0, 1), pl.ds(RING - 1, 1), pl.ds(COL0 + cols, 1)),
        )

        def edge_copy(n, back=1):
            dr, dc, sr, sc, tr, tc = edges[n]
            every = (pl.ds(0, 12),)
            return pltpu.make_async_remote_copy(
                src_ref=axl.at[(1,) + every + (sr, sc)], dst_ref=axl.at[(1,) + every + (tr, tc)],
                send_sem=edge_send.at[n], recv_sem=edge_recv.at[n],
                device_id=(r + dr * back, c + dc * back), device_id_type=MESH)

        for dr, dc, sr, sc, tr, tc in edges:
            @pl.when(jnp.logical_not(exists(-dr, -dc)))
            def _():
                axl[1, :, tr, tc, :] = jnp.zeros((12, tr.size, tc.size, LANES), F32)

        for dr, dc in around:
            @pl.when(jnp.logical_not(exists(dr, dc)))
            def _():
                tfv[(dr + 1) * 3 + dc + 1] = jnp.zeros((3, 4, rows, cols), F32)

        def blank(row_part, col_part):
            for buf in (xs, zs):
                shape = (4, 3, row_part.size, col_part.size, LANES)
                buf[:, :, row_part, col_part, :] = jnp.zeros(shape, F32)

        for flag, row_part, col_part in (
            (up, pl.ds(0, RING), pl.ds(0, WIDE)),
            (down, pl.ds(RING + rows, 1), pl.ds(0, WIDE)),
            (left, pl.ds(0, span), pl.ds(0, COL0)),
            (right, pl.ds(0, span), pl.ds(COL0 + cols, RING)),
        ):
            @pl.when(jnp.logical_not(flag))
            def _():
                blank(row_part, col_part)

        lane16 = lax.broadcasted_iota(jnp.int32, (8, cols), 1)
        sub8 = lax.broadcasted_iota(jnp.int32, (8, cols), 0)
        row_lane = lax.broadcasted_iota(jnp.int32, (1, LANES), 1)

        pl.semaphore_wait(barrier, greeted)

        def tf_copy(n, dr, dc):
            return pltpu.make_async_remote_copy(
                src_ref=tf, dst_ref=tfv.at[(1 - dr) * 3 + 1 - dc], send_sem=tf_send.at[n],
                recv_sem=tf_recv.at[n], device_id=(r + dr, c + dc), device_id_type=MESH)

        def tf_arrived(dr, dc):
            n = around.index((-dr, -dc))

            @pl.when(exists(dr, dc))
            def _():
                tf_copy(n, -dr, -dc).wait_recv()

        for dr, dc in ((1, 1), (1, -1), (-1, 1), (-1, -1), (1, 0), (-1, 0), (0, 1), (0, -1)):
            @pl.when(exists(dr, dc))
            def _():
                tf_copy(around.index((dr, dc)), dr, dc).start()

        for d in steps_xy:
            signal(known.at[0], at_xy(*d))
        signal(known.at[0], at_col(2))
        signal(known.at[0], at_col(-2))

        part_r = {1: (rows - 1, RING - 1, 1), 0: (0, RING, rows), -1: (0, RING + rows, 1)}
        part_c = {
            1: (cols - RING, COL0 - RING, RING), 0: (0, COL0, cols), -1: (0, COL0 + cols, RING)}

        def outer(dr, dc):
            n = around.index((dr, dc))
            sr, tr, nr = part_r[dr]
            sc, tc, nc = part_c[dc]
            src = (pl.ds(sr, nr), pl.ds(sc, nc), slice(None))
            dst = (pl.ds(tr, nr), pl.ds(tc, nc), slice(None))
            links = (pl.ds(1, 3) if dr > 0 else pl.ds(0, 4),)
            every = (slice(None),)
            return [
                pltpu.make_async_remote_copy(
                    src_ref=a.at[lead + src], dst_ref=b.at[lead + dst],
                    send_sem=pts_send.at[n, m], recv_sem=pts_recv.at[n, m],
                    device_id=(r + dr, c + dc), device_id_type=MESH)
                for m, (a, b, lead) in enumerate(
                    ((here, xs, links + every), (there, zs, links + every), (mask, ms, links)))
            ]

        for dr, dc in around:
            @pl.when(exists(dr, dc))
            def _():
                for copy in outer(dr, dc):
                    copy.start()

        def masks(d, i, lo, size):
            di, dj = LINKS[d]
            sub = lax.broadcasted_iota(jnp.int32, (size, LANES), 0)
            j = c * cols + sub + (lo - COL0)
            k = j + dj
            row = r * rows + i
            keep_row = (row >= 0) & (row + di < n_row * rows)
            keep = (j >= 0) & (j < n_col * cols) & (k >= 0) & (k < n_col * cols) & keep_row
            wm[d, RING + i, lo : lo + size, :] = jnp.where(
                keep, ms[d, RING + i, lo : lo + size, :].astype(F32), 0.0)

        own[1].wait()
        count = jnp.zeros((cols, LANES), F32)
        for d in range(4):
            for i in range(rows):
                masks(d, i, COL0, cols)
                count = count + wm[d, RING + i, COL0 : COL0 + cols, :]

        def all_sum(x):
            return jnp.sum(jnp.sum(x, axis=0, keepdims=True), axis=1, keepdims=True)

        def all_max(x):
            return jnp.max(jnp.max(x, axis=0, keepdims=True), axis=1, keepdims=True)

        count = all_sum(count)

        pl.semaphore_wait(known.at[0], 6)
        for device in (at_xy(0, 2), at_xy(0, -2), at_xy(2, 0), at_col(4), at_col(-4)):
            signal(known.at[1], device)

        own_lane = lane16 - sub8
        picks = (
            ((4, own_lane == -COL0), (3, own_lane == cols - COL0)),
            ((4, own_lane == 8 - COL0),),
            ((4, own_lane == 16 - COL0), (5, own_lane == 16 - COL0 - cols)),
        )

        def expand(i):
            base = 3 if 0 <= i < rows else (0 if i < 0 else 6)
            row = i % rows
            for k in range(12):
                for b, pick in enumerate(picks):
                    total = None
                    for slot, chosen in pick:
                        line = tfv[base + slot - 3, k // 4, k % 4, row : row + 1, :]
                        part = jnp.where(chosen, jnp.broadcast_to(line, (8, cols)), 0.0)
                        total = part if total is None else total + part
                    value = jnp.sum(total, axis=1, keepdims=True)
                    axl[0, k, RING + i, 8 * b : 8 * b + 8, :] = jnp.broadcast_to(value, (8, LANES))

        def errors(t, first, last, starts, carry=None):
            def body(i, carry):
                for lo in starts:
                    own_map = [axl[t, k, i, lo : lo + 8, :] for k in range(12)]
                    for d in range(4):
                        di, dj = LINKS[d]
                        x = [xs[d, n, i, lo : lo + 8, :] for n in range(3)]
                        z = [zs[d, n, i, lo : lo + 8, :] for n in range(3)]
                        err = None
                        for q in range(3):
                            far = [
                                axl[t, 4 * q + k, i + di, lo + dj : lo + dj + 8, :]
                                for k in range(4)
                            ]
                            y = far[3] + far[0] * z[0]
                            y = y + far[1] * z[1]
                            y = y + far[2] * z[2]
                            tm[d, q, i, lo : lo + 8, :] = y
                            a = own_map[4 * q + 3] + own_map[4 * q] * x[0]
                            a = a + own_map[4 * q + 1] * x[1]
                            a = a + own_map[4 * q + 2] * x[2]
                            hm[d, q, i, lo : lo + 8, :] = a
                            gap = a - y
                            err = gap * gap if err is None else err + gap * gap
                        errs[d, i, lo : lo + 8, :] = err
                        if carry is not None:
                            masked = wm[d, i, lo : lo + 8, :] * err
                            carry = (jnp.maximum(carry[0], masked), carry[1] + masked)
                return carry

            if carry is None:
                lax.fori_loop(first, last, lambda i, _: body(i, None) or 0, 0)
                return None
            return lax.fori_loop(first, last, body, carry)

        def weights(first, last, starts, scale):
            def body(i, _):
                for lo in starts:
                    for d in range(4):
                        at = (d, i, slice(lo, lo + 8))
                        wt[at] = wm[at] * (scale / (scale + errs[at]))
                return 0

            lax.fori_loop(first, last, body, 0)

        def moments(first, last, starts):
            def body(i, _):
                for lo in starts:
                    acc = [None] * 22
                    for e in range(8):
                        d = e % 4
                        di, dj = LINKS[d] if e >= 4 else (0, 0)
                        p, q = i - di, lo - dj
                        w = wt[d, p, q : q + 8, :]
                        mine, other = (xs, tm) if e < 4 else (zs, hm)
                        x = [mine[d, n, p, q : q + 8, :] for n in range(3)]
                        y = [other[d, n, p, q : q + 8, :] for n in range(3)]
                        wx = [w * v for v in x]
                        new = []
                        for a in range(3):
                            for b in range(a, 3):
                                new.append(wx[a] * x[b])
                            new.append(wx[a])
                        new.append(w)
                        for n in range(3):
                            wy = w * y[n]
                            new += [wy * v for v in x]
                            new.append(wy)
                        acc = [n if a is None else a + n for a, n in zip(acc, new)]
                    for n in range(22):
                        total = jnp.sum(acc[n], axis=1, keepdims=True)
                        sums[n, i, lo : lo + 8, :] = jnp.broadcast_to(total, (8, LANES))
                return 0

            lax.fori_loop(first, last, body, 0)

        own[0].wait()
        for spot in ((0, 1), (0, -1), (1, 0), (1, 1), (1, -1)):
            tf_arrived(*spot)
        for i in range(rows + 1):
            expand(i)
        own[2].wait()
        own[3].wait()

        def combine(block):
            return jnp.where(
                row_lane < 32, jnp.max(block, axis=0, keepdims=True),
                jnp.sum(block, axis=0, keepdims=True))

        def share(t, packed, stage, got, me, send_sem, recv_sem, targets):
            msg[t, stage] = packed
            got[t, pl.ds(me, 1), :] = packed
            for device in targets:
                pltpu.make_async_remote_copy(
                    src_ref=msg.at[t, stage], dst_ref=got.at[t, pl.ds(me, 1), :],
                    send_sem=send_sem.at[t], recv_sem=recv_sem.at[t],
                    device_id=device, device_id_type=MESH).start()

        def arrived(t, got, size, sem):
            block = got.at[t, pl.ds(0, size - 1), :]
            pltpu.make_async_copy(block, block, sem.at[t]).wait()

        col_targets = [at_col(s) for s in sorted(range(1, n_col), key=lambda s: -min(s, n_col - s))]
        plane = [(a, b) for a in range(NX) for b in range(NY) if a or b]
        plane.sort(key=lambda p: -(min(p[0], NX - p[0]) + min(p[1], NY - p[1])))
        row_targets = [at_xy(*p) for p in plane]

        own_starts = tuple(range(COL0, COL0 + cols, 8))
        for t in range(ITERS):
            zero = jnp.zeros((8, LANES), F32)
            top, total = errors(t, RING, RING + rows, own_starts, (zero, zero))
            top, total = all_max(top), all_sum(total)
            packed = jnp.where(row_lane < 32, top, jnp.where(row_lane < 64, total, count))
            if t == 0:
                pl.semaphore_wait(known.at[1], 5)
                signal(known.at[2], at_xy(0, 4))
            share(t, packed, 0, got_c, c, c_send, c_recv, col_targets)
            if t == 0:
                for spot in ((-1, 0), (-1, -1), (-1, 1)):
                    tf_arrived(*spot)
                for i in (-1, rows + 1):
                    expand(i)
                pl.semaphore_wait(known.at[2], 1)
            else:
                for n, (dr, dc, *_) in enumerate(edges):
                    @pl.when(exists(-dr, -dc))
                    def _():
                        edge_copy(n, -1).wait_recv()
                errors(t, RING - 1, RING, (2, 10, 18))
                errors(t, RING, RING + rows, (2, 18))
            arrived(t, got_c, n_col, c_recv)
            share(t, combine(got_c[t]), 1, got_r, r, r_send, r_recv, row_targets)
            if t == 0:
                for dr, dc in around:
                    @pl.when(exists(dr, dc))
                    def _():
                        for copy in outer(-dr, -dc):
                            copy.wait_recv()
                for d in range(4):
                    for i in range(-1, rows + 1):
                        if 0 <= i < rows:
                            masks(d, i, 0, 8)
                            masks(d, i, 16, 8)
                        else:
                            masks(d, i, 0, 24)
                errors(t, RING - 1, RING, (1, 9, 17))
                errors(t, RING + rows, RING + rows + 1, (1, 9, 17))
                errors(t, RING, RING + rows, (1, 17))
            arrived(t, got_r, n_row, r_recv)
            packed = combine(got_r[t])
            largest, total, number = packed[:, 0:1], packed[:, 32:33], packed[:, 64:65]
            mean = total / jnp.maximum(number, 1.0)
            scale = jnp.broadcast_to(0.25 * largest + 1e-6, (8, LANES))
            damping = DAMPING * mean + 1.0
            rec[t, 0] = jnp.broadcast_to(largest, (1, LANES))
            rec[t, 1] = jnp.broadcast_to(mean, (1, LANES))
            if t == 0:
                weights(RING - 1, span, (1, 9, 17), scale)
                blocks = [(RING, span, COL0 - 1, 24)]
            else:
                weights(RING - 1, RING + rows, (2, 10, 18), scale)
                blocks = [(RING, RING + rows, COL0, cols)]
            for first, last, lo, size in blocks:
                moments(first, last, range(lo, lo + size, 8))
            for i, lo, size in [(i, lo, size) for a, b, lo, size in blocks for i in range(a, b)]:
                damp = jnp.broadcast_to(damping, (size, LANES))
                old = [axl[t, k, i, lo : lo + size, :] for k in range(12)]
                gram, n = {}, 0
                for a in range(4):
                    for b in range(a, 4):
                        part = sums[n, i, lo : lo + size, :]
                        gram[a, b] = part + damp if a == b else part
                        n += 1
                cross = {}
                for q in range(3):
                    for b in range(4):
                        cross[q, b] = sums[n, i, lo : lo + size, :] + damp * old[4 * q + b]
                        n += 1
                new = solve(gram, cross)
                if t + 1 < ITERS:
                    for k in range(12):
                        axl[t + 1, k, i, lo : lo + size, :] = new[k]
                else:
                    lane = lax.broadcasted_iota(jnp.int32, (size, LANES), 1)
                    sub = lax.broadcasted_iota(jnp.int32, (size, LANES), 0)
                    for k in range(12):
                        line = jnp.sum(jnp.where(lane == sub, new[k], 0.0), axis=0, keepdims=True)
                        aligned[k // 4, k % 4, i - RING : i - RING + 1, :] = line[:, :cols]

            if t + 1 < ITERS:
                for n, (dr, dc, *_) in enumerate(edges):
                    @pl.when(exists(dr, dc))
                    def _():
                        edge_copy(n).start()

        a = lax.broadcasted_iota(jnp.int32, (2, 2), 1)
        b = lax.broadcasted_iota(jnp.int32, (2, 2), 0)
        stats[...] = jnp.where(
            b == 0,
            jnp.where(a == 0, rec[0, 0][:, :2], rec[1, 0][:, :2]),
            jnp.where(a == 0, rec[0, 1][:, :2], rec[1, 1][:, :2]))

        for dr, dc in around:
            @pl.when(exists(dr, dc))
            def _():
                tf_copy(around.index((dr, dc)), dr, dc).wait_send()
                for copy in outer(dr, dc):
                    copy.wait_send()
        for n, (dr, dc, *_) in enumerate(edges):
            @pl.when(exists(dr, dc))
            def _():
                edge_copy(n).wait_send()
        for t in range(ITERS):
            arrived(t, got_c, n_col, c_send)
            arrived(t, got_r, n_row, r_send)

    dma = pltpu.SemaphoreType.DMA
    vm = pltpu.VMEM
    grid = (span, WIDE, LANES)
    scratch = [
        vm((4, 3) + grid, F32),
        vm((4, 3) + grid, F32),
        vm((4,) + grid, jnp.int32),
        vm((4,) + grid, F32),
        vm((4,) + grid, F32),
        vm((4, 3) + grid, F32),
        vm((4, 3) + grid, F32),
        vm((4,) + grid, F32),
        vm((9, 3, 4, rows, cols), F32),
        vm((ITERS, 12, rows + 2 * RING, WIDE, LANES), F32),
        vm((22,) + grid, F32),
        vm((ITERS, 2, 1, LANES), F32),
        vm((ITERS, n_col, LANES), F32),
        vm((ITERS, n_row, LANES), F32),
        vm((ITERS, 2, 1, LANES), F32),
        dma((3,)), dma(()),
        dma((8, 3)), dma((8, 3)),
        dma((8,)), dma((8,)),
        dma((ITERS,)), dma((ITERS,)), dma((ITERS,)), dma((ITERS,)), dma((3,)), dma((3,)),
        pltpu.SemaphoreType.REGULAR((3,)),
    ]
    return kernel, scratch


def solution(mesh):
    n_row, n_col = mesh.shape["row"], mesh.shape["col"]

    def on_device(points_here, points_there, outlier_mask, transforms):
        rows, cols = transforms.shape[2:]
        kernel, scratch = make_kernel(n_row, n_col, rows, cols)
        hbm = pl.BlockSpec(memory_space=pltpu.HBM)
        return pl.pallas_call(
            kernel,
            out_shape=(
                jax.ShapeDtypeStruct(transforms.shape, F32),
                jax.ShapeDtypeStruct((2, ITERS), F32),
            ),
            in_specs=[hbm] * 4,
            out_specs=(pl.BlockSpec(memory_space=pltpu.VMEM),) * 2,
            scratch_shapes=scratch,
            compiler_params=pltpu.CompilerParams(collective_id=0, has_side_effects=True),
        )(points_here, points_there, outlier_mask, transforms)

    placed = (
        P(None, None, "row", "col", None),
        P(None, None, "row", "col", None),
        P(None, "row", "col", None),
        P(None, None, "row", "col"),
    )
    return jax.shard_map(
        on_device, mesh=mesh, in_specs=placed,
        out_specs=(P(None, None, "row", "col"), P()), check_vma=False)
```

```python
import jax
import jax.numpy as jnp
from jax import lax
from jax.experimental import pallas as pl
from jax.experimental.pallas import tpu as pltpu
from jax.sharding import PartitionSpec as P

ITERS = 2
MESH = pl.DeviceIdType.MESH
LINKS = ((0, 1), (1, 0), (1, 1), (1, -1))
DAMPING = 64.0
LANES = 128
RING = 2
WIDE = 32
COL0 = 3
NX, NY = 4, 8
F32 = jnp.float32


def solve(gram, cross):
    g = lambda a, b: gram[min(a, b), max(a, b)]
    low = [[None] * 4 for _ in range(4)]
    raw = [[None] * 4 for _ in range(4)]
    inv = [None] * 4
    for j in range(4):
        for i in range(j, 4):
            v = g(i, j)
            for k in range(j):
                v = v - low[i][k] * raw[j][k]
            raw[i][j] = v
        inv[j] = 1.0 / raw[j][j]
        for i in range(j + 1, 4):
            low[i][j] = raw[i][j] * inv[j]
    out = []
    for c in range(3):
        z = []
        for i in range(4):
            v = cross[c, i]
            for k in range(i):
                v = v - low[i][k] * z[k]
            z.append(v)
        s = [None] * 4
        for i in (3, 2, 1, 0):
            v = z[i] * inv[i]
            for k in range(i + 1, 4):
                v = v - low[k][i] * s[k]
            s[i] = v
        out.extend(s)
    return out


def make_kernel(n_row, n_col, rows, cols):
    around = [(a, b) for a in (-1, 0, 1) for b in (-1, 0, 1) if (a, b) != (0, 0)]
    span = rows + 2 * RING - 1

    def kernel(
        here, there, mask, tf, aligned, stats,
        xs, zs, ms, wm, wt, hm, tm, errs, tfv, axl, sums, msg, got_c, got_r, rec,
        own_sem, tf_sem, pts_send, pts_recv, tf_send, tf_recv,
        c_send, c_recv, r_send, r_recv, edge_send, edge_recv, known,
    ):
        r = lax.axis_index("row")
        c = lax.axis_index("col")
        x0, y0 = r // NY, lax.rem(r, NY)
        up, down, left, right = r > 0, r < n_row - 1, c > 0, c < n_col - 1
        side = {(-1, 0): up, (1, 0): down, (0, -1): left, (0, 1): right}

        def exists(dr, dc):
            if dr and dc:
                return side[dr, 0] & side[0, dc]
            return side[dr, dc]

        def at_col(s):
            return (r, lax.rem(c + s + n_col, n_col))

        def at_xy(dx, dy):
            return (lax.rem(x0 + dx + NX, NX) * NY + lax.rem(y0 + dy + NY, NY), c)

        def signal(sem, device):
            pl.semaphore_signal(sem, inc=1, device_id=device, device_id_type=MESH)

        one = lambda flag: flag.astype(jnp.int32)
        barrier = pltpu.get_barrier_semaphore()
        steps_xy = ((0, 1), (0, -1), (1, 0), (-1, 0))
        for d in steps_xy:
            signal(barrier, at_xy(*d))
        for s in (1, -1, 2, -2):
            signal(barrier, at_col(s))
        greeted = 8
        cross_up, cross_down = up & (y0 == 0), down & (y0 == NY - 1)
        for dr, dc, flag in (
            (-1, 0, cross_up), (1, 0, cross_down),
            (-1, -1, exists(-1, -1)), (-1, 1, exists(-1, 1)),
            (1, -1, exists(1, -1)), (1, 1, exists(1, 1)),
        ):
            greeted = greeted + one(flag)

            @pl.when(flag)
            def _():
                signal(barrier, (r + dr, c + dc))

        middle_r, middle_c = pl.ds(RING, rows), pl.ds(COL0, cols)
        own = [
            pltpu.make_async_copy(tf, tfv.at[4], tf_sem),
            pltpu.make_async_copy(mask, ms.at[:, middle_r, middle_c, :], own_sem.at[2]),
            pltpu.make_async_copy(here, xs.at[:, :, middle_r, middle_c, :], own_sem.at[0]),
            pltpu.make_async_copy(there, zs.at[:, :, middle_r, middle_c, :], own_sem.at[1]),
        ]
        for copy in own:
            copy.start()

        edges = (
            (1, 0, pl.ds(RING + rows - 1, 1), pl.ds(COL0, cols), pl.ds(RING - 1, 1), pl.ds(COL0, cols)),
            (1, 1, pl.ds(RING + rows - 1, 1), pl.ds(COL0 + cols - 1, 1),
             pl.ds(RING - 1, 1), pl.ds(COL0 - 1, 1)),
            (1, -1, pl.ds(RING + rows - 1, 1), pl.ds(COL0, 1), pl.ds(RING - 1, 1), pl.ds(COL0 + cols, 1)),
        )

        def edge_copy(n, back=1):
            dr, dc, sr, sc, tr, tc = edges[n]
            every = (pl.ds(0, 12),)
            return pltpu.make_async_remote_copy(
                src_ref=axl.at[(1,) + every + (sr, sc)], dst_ref=axl.at[(1,) + every + (tr, tc)],
                send_sem=edge_send.at[n], recv_sem=edge_recv.at[n],
                device_id=(r + dr * back, c + dc * back), device_id_type=MESH)

        for dr, dc, sr, sc, tr, tc in edges:
            @pl.when(jnp.logical_not(exists(-dr, -dc)))
            def _():
                axl[1, :, tr, tc, :] = jnp.zeros((12, tr.size, tc.size, LANES), F32)

        for dr, dc in around:
            @pl.when(jnp.logical_not(exists(dr, dc)))
            def _():
                tfv[(dr + 1) * 3 + dc + 1] = jnp.zeros((3, 4, rows, cols), F32)

        def blank(row_part, col_part):
            for buf in (xs, zs):
                shape = (4, 3, row_part.size, col_part.size, LANES)
                buf[:, :, row_part, col_part, :] = jnp.zeros(shape, F32)

        for flag, row_part, col_part in (
            (up, pl.ds(0, RING), pl.ds(0, WIDE)),
            (down, pl.ds(RING + rows, 1), pl.ds(0, WIDE)),
            (left, pl.ds(0, span), pl.ds(0, COL0)),
            (right, pl.ds(0, span), pl.ds(COL0 + cols, RING)),
        ):
            @pl.when(jnp.logical_not(flag))
            def _():
                blank(row_part, col_part)

        lane16 = lax.broadcasted_iota(jnp.int32, (8, cols), 1)
        sub8 = lax.broadcasted_iota(jnp.int32, (8, cols), 0)
        row_lane = lax.broadcasted_iota(jnp.int32, (1, LANES), 1)

        pl.semaphore_wait(barrier, greeted)

        def tf_copy(n, dr, dc):
            return pltpu.make_async_remote_copy(
                src_ref=tf, dst_ref=tfv.at[(1 - dr) * 3 + 1 - dc], send_sem=tf_send.at[n],
                recv_sem=tf_recv.at[n], device_id=(r + dr, c + dc), device_id_type=MESH)

        def tf_arrived(dr, dc):
            n = around.index((-dr, -dc))

            @pl.when(exists(dr, dc))
            def _():
                tf_copy(n, -dr, -dc).wait_recv()

        for dr, dc in ((1, 1), (1, -1), (-1, 1), (-1, -1), (1, 0), (-1, 0), (0, 1), (0, -1)):
            @pl.when(exists(dr, dc))
            def _():
                tf_copy(around.index((dr, dc)), dr, dc).start()

        for d in steps_xy:
            signal(known.at[0], at_xy(*d))
        signal(known.at[0], at_col(2))
        signal(known.at[0], at_col(-2))

        part_r = {1: (rows - 1, RING - 1, 1), 0: (0, RING, rows), -1: (0, RING + rows, 1)}
        part_c = {
            1: (cols - RING, COL0 - RING, RING), 0: (0, COL0, cols), -1: (0, COL0 + cols, RING)}

        def outer(dr, dc):
            n = around.index((dr, dc))
            sr, tr, nr = part_r[dr]
            sc, tc, nc = part_c[dc]
            src = (pl.ds(sr, nr), pl.ds(sc, nc), slice(None))
            dst = (pl.ds(tr, nr), pl.ds(tc, nc), slice(None))
            links = (pl.ds(1, 3) if dr > 0 else pl.ds(0, 4),)
            every = (slice(None),)
            return [
                pltpu.make_async_remote_copy(
                    src_ref=a.at[lead + src], dst_ref=b.at[lead + dst],
                    send_sem=pts_send.at[n, m], recv_sem=pts_recv.at[n, m],
                    device_id=(r + dr, c + dc), device_id_type=MESH)
                for m, (a, b, lead) in enumerate(
                    ((here, xs, links + every), (there, zs, links + every), (mask, ms, links)))
            ]

        for dr, dc in around:
            @pl.when(exists(dr, dc))
            def _():
                for copy in outer(dr, dc):
                    copy.start()

        def masks(d, i, lo, size):
            di, dj = LINKS[d]
            sub = lax.broadcasted_iota(jnp.int32, (size, LANES), 0)
            j = c * cols + sub + (lo - COL0)
            k = j + dj
            row = r * rows + i
            keep_row = (row >= 0) & (row + di < n_row * rows)
            keep = (j >= 0) & (j < n_col * cols) & (k >= 0) & (k < n_col * cols) & keep_row
            wm[d, RING + i, lo : lo + size, :] = jnp.where(
                keep, ms[d, RING + i, lo : lo + size, :].astype(F32), 0.0)

        own[1].wait()
        count = jnp.zeros((cols, LANES), F32)
        for d in range(4):
            for i in range(rows):
                masks(d, i, COL0, cols)
                count = count + wm[d, RING + i, COL0 : COL0 + cols, :]

        def all_sum(x):
            return jnp.sum(jnp.sum(x, axis=0, keepdims=True), axis=1, keepdims=True)

        def all_max(x):
            return jnp.max(jnp.max(x, axis=0, keepdims=True), axis=1, keepdims=True)

        count = all_sum(count)

        pl.semaphore_wait(known.at[0], 6)
        for device in (at_xy(0, 2), at_xy(0, -2), at_xy(2, 0), at_col(4), at_col(-4)):
            signal(known.at[1], device)

        own_lane = lane16 - sub8
        picks = (
            ((4, own_lane == -COL0), (3, own_lane == cols - COL0)),
            ((4, own_lane == 8 - COL0),),
            ((4, own_lane == 16 - COL0), (5, own_lane == 16 - COL0 - cols)),
        )

        def expand(i):
            base = 3 if 0 <= i < rows else (0 if i < 0 else 6)
            row = i % rows
            for k in range(12):
                for b, pick in enumerate(picks):
                    total = None
                    for slot, chosen in pick:
                        line = tfv[base + slot - 3, k // 4, k % 4, row : row + 1, :]
                        part = jnp.where(chosen, jnp.broadcast_to(line, (8, cols)), 0.0)
                        total = part if total is None else total + part
                    value = jnp.sum(total, axis=1, keepdims=True)
                    axl[0, k, RING + i, 8 * b : 8 * b + 8, :] = jnp.broadcast_to(value, (8, LANES))

        def errors(t, first, last, starts, carry=None):
            def body(i, carry):
                for lo in starts:
                    own_map = [axl[t, k, i, lo : lo + 8, :] for k in range(12)]
                    for d in range(4):
                        di, dj = LINKS[d]
                        x = [xs[d, n, i, lo : lo + 8, :] for n in range(3)]
                        z = [zs[d, n, i, lo : lo + 8, :] for n in range(3)]
                        err = None
                        for q in range(3):
                            far = [
                                axl[t, 4 * q + k, i + di, lo + dj : lo + dj + 8, :]
                                for k in range(4)
                            ]
                            y = far[3] + far[0] * z[0]
                            y = y + far[1] * z[1]
                            y = y + far[2] * z[2]
                            tm[d, q, i, lo : lo + 8, :] = y
                            a = own_map[4 * q + 3] + own_map[4 * q] * x[0]
                            a = a + own_map[4 * q + 1] * x[1]
                            a = a + own_map[4 * q + 2] * x[2]
                            hm[d, q, i, lo : lo + 8, :] = a
                            gap = a - y
                            err = gap * gap if err is None else err + gap * gap
                        errs[d, i, lo : lo + 8, :] = err
                        if carry is not None:
                            masked = wm[d, i, lo : lo + 8, :] * err
                            carry = (jnp.maximum(carry[0], masked), carry[1] + masked)
                return carry

            if carry is None:
                lax.fori_loop(first, last, lambda i, _: body(i, None) or 0, 0)
                return None
            return lax.fori_loop(first, last, body, carry)

        def weights(first, last, starts, scale):
            def body(i, _):
                for lo in starts:
                    for d in range(4):
                        at = (d, i, slice(lo, lo + 8))
                        wt[at] = wm[at] * (scale / (scale + errs[at]))
                return 0

            lax.fori_loop(first, last, body, 0)

        def moments(first, last, starts):
            def body(i, _):
                for lo in starts:
                    acc = [None] * 22
                    for e in range(8):
                        d = e % 4
                        di, dj = LINKS[d] if e >= 4 else (0, 0)
                        p, q = i - di, lo - dj
                        w = wt[d, p, q : q + 8, :]
                        mine, other = (xs, tm) if e < 4 else (zs, hm)
                        x = [mine[d, n, p, q : q + 8, :] for n in range(3)]
                        y = [other[d, n, p, q : q + 8, :] for n in range(3)]
                        wx = [w * v for v in x]
                        new = []
                        for a in range(3):
                            for b in range(a, 3):
                                new.append(wx[a] * x[b])
                            new.append(wx[a])
                        new.append(w)
                        for n in range(3):
                            wy = w * y[n]
                            new += [wy * v for v in x]
                            new.append(wy)
                        acc = [n if a is None else a + n for a, n in zip(acc, new)]
                    for n in range(22):
                        total = jnp.sum(acc[n], axis=1, keepdims=True)
                        sums[n, i, lo : lo + 8, :] = jnp.broadcast_to(total, (8, LANES))
                return 0

            lax.fori_loop(first, last, body, 0, unroll=True)

        own[0].wait()
        for spot in ((0, 1), (0, -1), (1, 0), (1, 1), (1, -1)):
            tf_arrived(*spot)
        for i in range(rows + 1):
            expand(i)
        own[2].wait()
        own[3].wait()

        def combine(block):
            return jnp.where(
                row_lane < 32, jnp.max(block, axis=0, keepdims=True),
                jnp.sum(block, axis=0, keepdims=True))

        def share(t, packed, stage, got, me, send_sem, recv_sem, targets):
            msg[t, stage] = packed
            got[t, pl.ds(me, 1), :] = packed
            for device in targets:
                pltpu.make_async_remote_copy(
                    src_ref=msg.at[t, stage], dst_ref=got.at[t, pl.ds(me, 1), :],
                    send_sem=send_sem.at[t], recv_sem=recv_sem.at[t],
                    device_id=device, device_id_type=MESH).start()

        def arrived(t, got, size, sem):
            block = got.at[t, pl.ds(0, size - 1), :]
            pltpu.make_async_copy(block, block, sem.at[t]).wait()

        col_targets = [at_col(s) for s in sorted(range(1, n_col), key=lambda s: -min(s, n_col - s))]
        plane = [(a, b) for a in range(NX) for b in range(NY) if a or b]
        plane.sort(key=lambda p: -(min(p[0], NX - p[0]) + min(p[1], NY - p[1])))
        row_targets = [at_xy(*p) for p in plane]

        own_starts = tuple(range(COL0, COL0 + cols, 8))
        for t in range(ITERS):
            zero = jnp.zeros((8, LANES), F32)
            top, total = errors(t, RING, RING + rows, own_starts, (zero, zero))
            top, total = all_max(top), all_sum(total)
            packed = jnp.where(row_lane < 32, top, jnp.where(row_lane < 64, total, count))
            if t == 0:
                pl.semaphore_wait(known.at[1], 5)
                signal(known.at[2], at_xy(0, 4))
            share(t, packed, 0, got_c, c, c_send, c_recv, col_targets)
            if t == 0:
                for spot in ((-1, 0), (-1, -1), (-1, 1)):
                    tf_arrived(*spot)
                for i in (-1, rows + 1):
                    expand(i)
                pl.semaphore_wait(known.at[2], 1)
            else:
                for n, (dr, dc, *_) in enumerate(edges):
                    @pl.when(exists(-dr, -dc))
                    def _():
                        edge_copy(n, -1).wait_recv()
                errors(t, RING - 1, RING, (2, 10, 18))
                errors(t, RING, RING + rows, (2, 18))
            arrived(t, got_c, n_col, c_recv)
            share(t, combine(got_c[t]), 1, got_r, r, r_send, r_recv, row_targets)
            if t == 0:
                for dr, dc in around:
                    @pl.when(exists(dr, dc))
                    def _():
                        for copy in outer(-dr, -dc):
                            copy.wait_recv()
                for d in range(4):
                    for i in range(-1, rows + 1):
                        if 0 <= i < rows:
                            masks(d, i, 0, 8)
                            masks(d, i, 16, 8)
                        else:
                            masks(d, i, 0, 24)
                errors(t, RING - 1, RING, (1, 9, 17))
                errors(t, RING + rows, RING + rows + 1, (1, 9, 17))
                errors(t, RING, RING + rows, (1, 17))
            arrived(t, got_r, n_row, r_recv)
            packed = combine(got_r[t])
            largest, total, number = packed[:, 0:1], packed[:, 32:33], packed[:, 64:65]
            mean = total / jnp.maximum(number, 1.0)
            scale = jnp.broadcast_to(0.25 * largest + 1e-6, (8, LANES))
            damping = DAMPING * mean + 1.0
            rec[t, 0] = jnp.broadcast_to(largest, (1, LANES))
            rec[t, 1] = jnp.broadcast_to(mean, (1, LANES))
            if t == 0:
                weights(RING - 1, span, (1, 9, 17), scale)
                blocks = [(RING, span, COL0 - 1, 24)]
            else:
                weights(RING - 1, RING + rows, (2, 10, 18), scale)
                blocks = [(RING, RING + rows, COL0, cols)]
            for first, last, lo, size in blocks:
                moments(first, last, range(lo, lo + size, 8))
            for i, lo, size in [(i, lo, size) for a, b, lo, size in blocks for i in range(a, b)]:
                damp = jnp.broadcast_to(damping, (size, LANES))
                old = [axl[t, k, i, lo : lo + size, :] for k in range(12)]
                gram, n = {}, 0
                for a in range(4):
                    for b in range(a, 4):
                        part = sums[n, i, lo : lo + size, :]
                        gram[a, b] = part + damp if a == b else part
                        n += 1
                cross = {}
                for q in range(3):
                    for b in range(4):
                        cross[q, b] = sums[n, i, lo : lo + size, :] + damp * old[4 * q + b]
                        n += 1
                new = solve(gram, cross)
                if t + 1 < ITERS:
                    for k in range(12):
                        axl[t + 1, k, i, lo : lo + size, :] = new[k]
                else:
                    lane = lax.broadcasted_iota(jnp.int32, (size, LANES), 1)
                    sub = lax.broadcasted_iota(jnp.int32, (size, LANES), 0)
                    for k in range(12):
                        line = jnp.sum(jnp.where(lane == sub, new[k], 0.0), axis=0, keepdims=True)
                        aligned[k // 4, k % 4, i - RING : i - RING + 1, :] = line[:, :cols]

            if t + 1 < ITERS:
                for n, (dr, dc, *_) in enumerate(edges):
                    @pl.when(exists(dr, dc))
                    def _():
                        edge_copy(n).start()

        a = lax.broadcasted_iota(jnp.int32, (2, 2), 1)
        b = lax.broadcasted_iota(jnp.int32, (2, 2), 0)
        stats[...] = jnp.where(
            b == 0,
            jnp.where(a == 0, rec[0, 0][:, :2], rec[1, 0][:, :2]),
            jnp.where(a == 0, rec[0, 1][:, :2], rec[1, 1][:, :2]))

        for dr, dc in around:
            @pl.when(exists(dr, dc))
            def _():
                tf_copy(around.index((dr, dc)), dr, dc).wait_send()
                for copy in outer(dr, dc):
                    copy.wait_send()
        for n, (dr, dc, *_) in enumerate(edges):
            @pl.when(exists(dr, dc))
            def _():
                edge_copy(n).wait_send()
        for t in range(ITERS):
            arrived(t, got_c, n_col, c_send)
            arrived(t, got_r, n_row, r_send)

    dma = pltpu.SemaphoreType.DMA
    vm = pltpu.VMEM
    grid = (span, WIDE, LANES)
    scratch = [
        vm((4, 3) + grid, F32),
        vm((4, 3) + grid, F32),
        vm((4,) + grid, jnp.int32),
        vm((4,) + grid, F32),
        vm((4,) + grid, F32),
        vm((4, 3) + grid, F32),
        vm((4, 3) + grid, F32),
        vm((4,) + grid, F32),
        vm((9, 3, 4, rows, cols), F32),
        vm((ITERS, 12, rows + 2 * RING, WIDE, LANES), F32),
        vm((22,) + grid, F32),
        vm((ITERS, 2, 1, LANES), F32),
        vm((ITERS, n_col, LANES), F32),
        vm((ITERS, n_row, LANES), F32),
        vm((ITERS, 2, 1, LANES), F32),
        dma((3,)), dma(()),
        dma((8, 3)), dma((8, 3)),
        dma((8,)), dma((8,)),
        dma((ITERS,)), dma((ITERS,)), dma((ITERS,)), dma((ITERS,)), dma((3,)), dma((3,)),
        pltpu.SemaphoreType.REGULAR((3,)),
    ]
    return kernel, scratch


def solution(mesh):
    n_row, n_col = mesh.shape["row"], mesh.shape["col"]

    def on_device(points_here, points_there, outlier_mask, transforms):
        rows, cols = transforms.shape[2:]
        kernel, scratch = make_kernel(n_row, n_col, rows, cols)
        hbm = pl.BlockSpec(memory_space=pltpu.HBM)
        return pl.pallas_call(
            kernel,
            out_shape=(
                pltpu.VMEM(transforms.shape, F32),
                pltpu.VMEM((2, ITERS), F32),
            ),
            in_specs=[hbm] * 4,
            out_specs=(pl.BlockSpec(memory_space=pltpu.VMEM),) * 2,
            scratch_shapes=scratch,
            compiler_params=pltpu.CompilerParams(collective_id=0, has_side_effects=True),
        )(points_here, points_there, outlier_mask, transforms)

    placed = (
        P(None, None, "row", "col", None),
        P(None, None, "row", "col", None),
        P(None, "row", "col", None),
        P(None, None, "row", "col"),
    )
    return jax.shard_map(
        on_device, mesh=mesh, in_specs=placed,
        out_specs=(P(None, None, "row", "col"), P()), check_vma=False)
```

```python
import jax
import jax.numpy as jnp
from jax import lax
from jax.experimental import pallas as pl
from jax.experimental.pallas import tpu as pltpu
from jax.sharding import PartitionSpec as P

ITERS = 2
MESH = pl.DeviceIdType.MESH
LINKS = ((0, 1), (1, 0), (1, 1), (1, -1))
DAMPING = 64.0
LANES = 128
RING = 2
WIDE = 32
COL0 = 3
NX, NY = 4, 8
F32 = jnp.float32


def solve(gram, cross):
    g = lambda a, b: gram[min(a, b), max(a, b)]
    low = [[None] * 4 for _ in range(4)]
    raw = [[None] * 4 for _ in range(4)]
    inv = [None] * 4
    for j in range(4):
        for i in range(j, 4):
            v = g(i, j)
            for k in range(j):
                v = v - low[i][k] * raw[j][k]
            raw[i][j] = v
        inv[j] = 1.0 / raw[j][j]
        for i in range(j + 1, 4):
            low[i][j] = raw[i][j] * inv[j]
    out = []
    for c in range(3):
        z = []
        for i in range(4):
            v = cross[c, i]
            for k in range(i):
                v = v - low[i][k] * z[k]
            z.append(v)
        s = [None] * 4
        for i in (3, 2, 1, 0):
            v = z[i] * inv[i]
            for k in range(i + 1, 4):
                v = v - low[k][i] * s[k]
            s[i] = v
        out.extend(s)
    return out


def make_kernel(n_row, n_col, rows, cols):
    around = [(a, b) for a in (-1, 0, 1) for b in (-1, 0, 1) if (a, b) != (0, 0)]
    span = rows + 2 * RING - 1

    def kernel(
        here, there, mask, tf, aligned, stats,
        xs, zs, ms, wm, wt, hm, tm, errs, tfv, axl, sums, msg, got_c, got_r, rec,
        own_sem, tf_sem, pts_send, pts_recv, tf_send, tf_recv,
        c_send, c_recv, r_send, r_recv, edge_send, edge_recv, known,
    ):
        r = lax.axis_index("row")
        c = lax.axis_index("col")
        x0, y0 = r // NY, lax.rem(r, NY)
        up, down, left, right = r > 0, r < n_row - 1, c > 0, c < n_col - 1
        side = {(-1, 0): up, (1, 0): down, (0, -1): left, (0, 1): right}

        def exists(dr, dc):
            if dr and dc:
                return side[dr, 0] & side[0, dc]
            return side[dr, dc]

        def at_col(s):
            return (r, lax.rem(c + s + n_col, n_col))

        def at_xy(dx, dy):
            return (lax.rem(x0 + dx + NX, NX) * NY + lax.rem(y0 + dy + NY, NY), c)

        def signal(sem, device):
            pl.semaphore_signal(sem, inc=1, device_id=device, device_id_type=MESH)

        one = lambda flag: flag.astype(jnp.int32)
        barrier = pltpu.get_barrier_semaphore()
        steps_xy = ((0, 1), (0, -1), (1, 0), (-1, 0))
        for d in steps_xy:
            signal(barrier, at_xy(*d))
        for s in (1, -1, 2, -2):
            signal(barrier, at_col(s))
        greeted = 8
        cross_up, cross_down = up & (y0 == 0), down & (y0 == NY - 1)
        for dr, dc, flag in (
            (-1, 0, cross_up), (1, 0, cross_down),
            (-1, -1, exists(-1, -1)), (-1, 1, exists(-1, 1)),
            (1, -1, exists(1, -1)), (1, 1, exists(1, 1)),
        ):
            greeted = greeted + one(flag)

            @pl.when(flag)
            def _():
                signal(barrier, (r + dr, c + dc))

        middle_r, middle_c = pl.ds(RING, rows), pl.ds(COL0, cols)
        own = [
            pltpu.make_async_copy(tf, tfv.at[4], tf_sem),
            pltpu.make_async_copy(mask, ms.at[:, middle_r, middle_c, :], own_sem.at[2]),
            pltpu.make_async_copy(here, xs.at[:, :, middle_r, middle_c, :], own_sem.at[0]),
            pltpu.make_async_copy(there, zs.at[:, :, middle_r, middle_c, :], own_sem.at[1]),
        ]
        for copy in own:
            copy.start()

        edges = (
            (1, 0, pl.ds(RING + rows - 1, 1), pl.ds(COL0, cols), pl.ds(RING - 1, 1), pl.ds(COL0, cols)),
            (1, 1, pl.ds(RING + rows - 1, 1), pl.ds(COL0 + cols - 1, 1),
             pl.ds(RING - 1, 1), pl.ds(COL0 - 1, 1)),
            (1, -1, pl.ds(RING + rows - 1, 1), pl.ds(COL0, 1), pl.ds(RING - 1, 1), pl.ds(COL0 + cols, 1)),
        )

        def edge_copy(n, back=1):
            dr, dc, sr, sc, tr, tc = edges[n]
            every = (pl.ds(0, 12),)
            return pltpu.make_async_remote_copy(
                src_ref=axl.at[(1,) + every + (sr, sc)], dst_ref=axl.at[(1,) + every + (tr, tc)],
                send_sem=edge_send.at[n], recv_sem=edge_recv.at[n],
                device_id=(r + dr * back, c + dc * back), device_id_type=MESH)

        for dr, dc, sr, sc, tr, tc in edges:
            @pl.when(jnp.logical_not(exists(-dr, -dc)))
            def _():
                axl[1, :, tr, tc, :] = jnp.zeros((12, tr.size, tc.size, LANES), F32)

        for dr, dc in around:
            @pl.when(jnp.logical_not(exists(dr, dc)))
            def _():
                tfv[(dr + 1) * 3 + dc + 1] = jnp.zeros((3, 4, rows, cols), F32)

        def blank(row_part, col_part):
            for buf in (xs, zs):
                shape = (4, 3, row_part.size, col_part.size, LANES)
                buf[:, :, row_part, col_part, :] = jnp.zeros(shape, F32)

        for flag, row_part, col_part in (
            (up, pl.ds(0, RING), pl.ds(0, WIDE)),
            (down, pl.ds(RING + rows, 1), pl.ds(0, WIDE)),
            (left, pl.ds(0, span), pl.ds(0, COL0)),
            (right, pl.ds(0, span), pl.ds(COL0 + cols, RING)),
        ):
            @pl.when(jnp.logical_not(flag))
            def _():
                blank(row_part, col_part)

        lane16 = lax.broadcasted_iota(jnp.int32, (8, cols), 1)
        sub8 = lax.broadcasted_iota(jnp.int32, (8, cols), 0)
        row_lane = lax.broadcasted_iota(jnp.int32, (1, LANES), 1)

        own_lane = lane16 - sub8
        picks = (
            ((4, own_lane == -COL0), (3, own_lane == cols - COL0)),
            ((4, own_lane == 8 - COL0),),
            ((4, own_lane == 16 - COL0), (5, own_lane == 16 - COL0 - cols)),
        )

        def expand(i, inner=False):
            base = 3 if 0 <= i < rows else (0 if i < 0 else 6)
            row = i % rows
            for k in range(12):
                for b, pick in enumerate(picks):
                    total = None
                    for slot, chosen in (pick[:1] if inner else pick):
                        line = tfv[base + slot - 3, k // 4, k % 4, row : row + 1, :]
                        part = jnp.where(chosen, jnp.broadcast_to(line, (8, cols)), 0.0)
                        total = part if total is None else total + part
                    value = jnp.sum(total, axis=1, keepdims=True)
                    axl[0, k, RING + i, 8 * b : 8 * b + 8, :] = jnp.broadcast_to(value, (8, LANES))

        def column(slot, first_lane, col):
            for k in range(12):
                value = tfv[slot, k // 4, k % 4][:, first_lane : first_lane + 1]
                value = jnp.broadcast_to(value, (rows, LANES))
                for i in range(rows):
                    axl[0, k, RING + i, COL0 + col : COL0 + col + 1, :] = value[i : i + 1, :]

        own[0].wait()
        for i in range(rows):
            expand(i, True)

        pl.semaphore_wait(barrier, greeted)

        def tf_copy(n, dr, dc):
            return pltpu.make_async_remote_copy(
                src_ref=tfv.at[4], dst_ref=tfv.at[(1 - dr) * 3 + 1 - dc], send_sem=tf_send.at[n],
                recv_sem=tf_recv.at[n], device_id=(r + dr, c + dc), device_id_type=MESH)

        def tf_arrived(dr, dc):
            n = around.index((-dr, -dc))

            @pl.when(exists(dr, dc))
            def _():
                tf_copy(n, -dr, -dc).wait_recv()

        for dr, dc in ((-1, 1), (-1, -1), (-1, 0), (0, 1), (0, -1), (1, 1), (1, -1), (1, 0)):
            @pl.when(exists(dr, dc))
            def _():
                tf_copy(around.index((dr, dc)), dr, dc).start()

        for d in steps_xy:
            signal(known.at[0], at_xy(*d))
        signal(known.at[0], at_col(2))
        signal(known.at[0], at_col(-2))

        part_r = {1: (rows - 1, RING - 1, 1), 0: (0, RING, rows), -1: (0, RING + rows, 1)}
        part_c = {
            1: (cols - RING, COL0 - RING, RING), 0: (0, COL0, cols), -1: (0, COL0 + cols, RING)}

        def outer(dr, dc):
            n = around.index((dr, dc))
            sr, tr, nr = part_r[dr]
            sc, tc, nc = part_c[dc]
            src = (pl.ds(sr, nr), pl.ds(sc, nc), slice(None))
            dst = (pl.ds(tr, nr), pl.ds(tc, nc), slice(None))
            links = (pl.ds(1, 3) if dr > 0 else pl.ds(0, 4),)
            every = (slice(None),)
            return [
                pltpu.make_async_remote_copy(
                    src_ref=a.at[lead + src], dst_ref=b.at[lead + dst],
                    send_sem=pts_send.at[n, m], recv_sem=pts_recv.at[n, m],
                    device_id=(r + dr, c + dc), device_id_type=MESH)
                for m, (a, b, lead) in enumerate(
                    ((here, xs, links + every), (there, zs, links + every), (mask, ms, links)))
            ]

        for dr, dc in around:
            @pl.when(exists(dr, dc))
            def _():
                for copy in outer(dr, dc):
                    copy.start()

        def masks(d, i, lo, size):
            di, dj = LINKS[d]
            sub = lax.broadcasted_iota(jnp.int32, (size, LANES), 0)
            j = c * cols + sub + (lo - COL0)
            k = j + dj
            row = r * rows + i
            keep_row = (row >= 0) & (row + di < n_row * rows)
            keep = (j >= 0) & (j < n_col * cols) & (k >= 0) & (k < n_col * cols) & keep_row
            wm[d, RING + i, lo : lo + size, :] = jnp.where(
                keep, ms[d, RING + i, lo : lo + size, :].astype(F32), 0.0)

        own[1].wait()
        count = jnp.zeros((cols, LANES), F32)
        for d in range(4):
            for i in range(rows):
                masks(d, i, COL0, cols)
                count = count + wm[d, RING + i, COL0 : COL0 + cols, :]

        def all_sum(x):
            return jnp.sum(jnp.sum(x, axis=0, keepdims=True), axis=1, keepdims=True)

        def all_max(x):
            return jnp.max(jnp.max(x, axis=0, keepdims=True), axis=1, keepdims=True)

        count = all_sum(count)

        pl.semaphore_wait(known.at[0], 6)
        for device in (at_xy(0, 2), at_xy(0, -2), at_xy(2, 0), at_col(4), at_col(-4)):
            signal(known.at[1], device)


        def errors(t, first, last, starts, carry=None):
            def body(i, carry):
                for lo in starts:
                    own_map = [axl[t, k, i, lo : lo + 8, :] for k in range(12)]
                    for d in range(4):
                        di, dj = LINKS[d]
                        x = [xs[d, n, i, lo : lo + 8, :] for n in range(3)]
                        z = [zs[d, n, i, lo : lo + 8, :] for n in range(3)]
                        err = None
                        for q in range(3):
                            far = [
                                axl[t, 4 * q + k, i + di, lo + dj : lo + dj + 8, :]
                                for k in range(4)
                            ]
                            y = far[3] + far[0] * z[0]
                            y = y + far[1] * z[1]
                            y = y + far[2] * z[2]
                            tm[d, q, i, lo : lo + 8, :] = y
                            a = own_map[4 * q + 3] + own_map[4 * q] * x[0]
                            a = a + own_map[4 * q + 1] * x[1]
                            a = a + own_map[4 * q + 2] * x[2]
                            hm[d, q, i, lo : lo + 8, :] = a
                            gap = a - y
                            err = gap * gap if err is None else err + gap * gap
                        errs[d, i, lo : lo + 8, :] = err
                        if carry is not None:
                            masked = wm[d, i, lo : lo + 8, :] * err
                            carry = (jnp.maximum(carry[0], masked), carry[1] + masked)
                return carry

            if carry is None:
                lax.fori_loop(first, last, lambda i, _: body(i, None) or 0, 0)
                return None
            return lax.fori_loop(first, last, body, carry)

        def weights(first, last, starts, scale):
            def body(i, _):
                for lo in starts:
                    for d in range(4):
                        at = (d, i, slice(lo, lo + 8))
                        wt[at] = wm[at] * (scale / (scale + errs[at]))
                return 0

            lax.fori_loop(first, last, body, 0)

        def moments(first, last, starts):
            def body(i, _):
                for lo in starts:
                    acc = [None] * 22
                    for e in range(8):
                        d = e % 4
                        di, dj = LINKS[d] if e >= 4 else (0, 0)
                        p, q = i - di, lo - dj
                        w = wt[d, p, q : q + 8, :]
                        mine, other = (xs, tm) if e < 4 else (zs, hm)
                        x = [mine[d, n, p, q : q + 8, :] for n in range(3)]
                        y = [other[d, n, p, q : q + 8, :] for n in range(3)]
                        wx = [w * v for v in x]
                        new = []
                        for a in range(3):
                            for b in range(a, 3):
                                new.append(wx[a] * x[b])
                            new.append(wx[a])
                        new.append(w)
                        for n in range(3):
                            wy = w * y[n]
                            new += [wy * v for v in x]
                            new.append(wy)
                        acc = [n if a is None else a + n for a, n in zip(acc, new)]
                    for n in range(22):
                        total = jnp.sum(acc[n], axis=1, keepdims=True)
                        sums[n, i, lo : lo + 8, :] = jnp.broadcast_to(total, (8, LANES))
                return 0

            lax.fori_loop(first, last, body, 0, unroll=True)

        for spot in ((0, 1), (0, -1), (1, 0), (1, 1), (1, -1)):
            tf_arrived(*spot)
        expand(rows)
        column(3, cols - 1, -1)
        column(5, 0, cols)
        own[2].wait()
        own[3].wait()

        def combine(block):
            return jnp.where(
                row_lane < 32, jnp.max(block, axis=0, keepdims=True),
                jnp.sum(block, axis=0, keepdims=True))

        def share(t, packed, stage, got, me, send_sem, recv_sem, targets):
            msg[t, stage] = packed
            got[t, pl.ds(me, 1), :] = packed
            for device in targets:
                pltpu.make_async_remote_copy(
                    src_ref=msg.at[t, stage], dst_ref=got.at[t, pl.ds(me, 1), :],
                    send_sem=send_sem.at[t], recv_sem=recv_sem.at[t],
                    device_id=device, device_id_type=MESH).start()

        def arrived(t, got, size, sem):
            block = got.at[t, pl.ds(0, size - 1), :]
            pltpu.make_async_copy(block, block, sem.at[t]).wait()

        col_targets = [at_col(s) for s in sorted(range(1, n_col), key=lambda s: -min(s, n_col - s))]
        plane = [(a, b) for a in range(NX) for b in range(NY) if a or b]
        plane.sort(key=lambda p: -(min(p[0], NX - p[0]) + min(p[1], NY - p[1])))
        row_targets = [at_xy(*p) for p in plane]

        own_starts = tuple(range(COL0, COL0 + cols, 8))
        for t in range(ITERS):
            zero = jnp.zeros((8, LANES), F32)
            top, total = errors(t, RING, RING + rows, own_starts, (zero, zero))
            top, total = all_max(top), all_sum(total)
            packed = jnp.where(row_lane < 32, top, jnp.where(row_lane < 64, total, count))
            if t == 0:
                pl.semaphore_wait(known.at[1], 5)
                signal(known.at[2], at_xy(0, 4))
            share(t, packed, 0, got_c, c, c_send, c_recv, col_targets)
            if t == 0:
                for spot in ((-1, 0), (-1, -1), (-1, 1)):
                    tf_arrived(*spot)
                for i in (-1, rows + 1):
                    expand(i)
                column(3, cols - 2, -2)
                column(5, 1, cols + 1)
                pl.semaphore_wait(known.at[2], 1)
            else:
                for n, (dr, dc, *_) in enumerate(edges):
                    @pl.when(exists(-dr, -dc))
                    def _():
                        edge_copy(n, -1).wait_recv()
                errors(t, RING - 1, RING, (2, 10, 18))
                errors(t, RING, RING + rows, (2, 18))
            arrived(t, got_c, n_col, c_recv)
            share(t, combine(got_c[t]), 1, got_r, r, r_send, r_recv, row_targets)
            if t == 0:
                for dr, dc in around:
                    @pl.when(exists(dr, dc))
                    def _():
                        for copy in outer(-dr, -dc):
                            copy.wait_recv()
                for d in range(4):
                    for i in range(-1, rows + 1):
                        if 0 <= i < rows:
                            masks(d, i, 0, 8)
                            masks(d, i, 16, 8)
                        else:
                            masks(d, i, 0, 24)
                errors(t, RING - 1, RING, (1, 9, 17))
                errors(t, RING + rows, RING + rows + 1, (1, 9, 17))
                errors(t, RING, RING + rows, (1, 17))
            if t + 1 == ITERS:
                for dr, dc in around:
                    @pl.when(exists(dr, dc))
                    def _():
                        tf_copy(around.index((dr, dc)), dr, dc).wait_send()
                        for copy in outer(dr, dc):
                            copy.wait_send()
                for n, (dr, dc, *_) in enumerate(edges):
                    @pl.when(exists(dr, dc))
                    def _():
                        edge_copy(n).wait_send()
                arrived(0, got_c, n_col, c_send)
                arrived(0, got_r, n_row, r_send)
                arrived(t, got_c, n_col, c_send)
            arrived(t, got_r, n_row, r_recv)
            packed = combine(got_r[t])
            largest, total, number = packed[:, 0:1], packed[:, 32:33], packed[:, 64:65]
            mean = total / jnp.maximum(number, 1.0)
            scale = jnp.broadcast_to(0.25 * largest + 1e-6, (8, LANES))
            damping = DAMPING * mean + 1.0
            rec[t, 0] = jnp.broadcast_to(largest, (1, LANES))
            rec[t, 1] = jnp.broadcast_to(mean, (1, LANES))
            if t == 0:
                weights(RING - 1, span, (1, 9, 17), scale)
                blocks = [(RING, span, COL0 - 1, 24)]
            else:
                weights(RING - 1, RING + rows, (2, 10, 18), scale)
                blocks = [(RING, RING + rows, COL0, cols)]
            for first, last, lo, size in blocks:
                moments(first, last, range(lo, lo + size, 8))
            for i, lo, size in [(i, lo, size) for a, b, lo, size in blocks for i in range(a, b)]:
                damp = jnp.broadcast_to(damping, (size, LANES))
                old = [axl[t, k, i, lo : lo + size, :] for k in range(12)]
                gram, n = {}, 0
                for a in range(4):
                    for b in range(a, 4):
                        part = sums[n, i, lo : lo + size, :]
                        gram[a, b] = part + damp if a == b else part
                        n += 1
                cross = {}
                for q in range(3):
                    for b in range(4):
                        cross[q, b] = sums[n, i, lo : lo + size, :] + damp * old[4 * q + b]
                        n += 1
                new = solve(gram, cross)
                if t + 1 < ITERS:
                    for k in range(12):
                        axl[t + 1, k, i, lo : lo + size, :] = new[k]
                else:
                    lane = lax.broadcasted_iota(jnp.int32, (size, LANES), 1)
                    sub = lax.broadcasted_iota(jnp.int32, (size, LANES), 0)
                    for k in range(12):
                        line = jnp.sum(jnp.where(lane == sub, new[k], 0.0), axis=0, keepdims=True)
                        aligned[k // 4, k % 4, i - RING : i - RING + 1, :] = line[:, :cols]

            if t + 1 < ITERS:
                for n, (dr, dc, *_) in enumerate(edges):
                    @pl.when(exists(dr, dc))
                    def _():
                        edge_copy(n).start()

        a = lax.broadcasted_iota(jnp.int32, (2, 2), 1)
        b = lax.broadcasted_iota(jnp.int32, (2, 2), 0)
        stats[...] = jnp.where(
            b == 0,
            jnp.where(a == 0, rec[0, 0][:, :2], rec[1, 0][:, :2]),
            jnp.where(a == 0, rec[0, 1][:, :2], rec[1, 1][:, :2]))

        arrived(ITERS - 1, got_r, n_row, r_send)

    dma = pltpu.SemaphoreType.DMA
    vm = pltpu.VMEM
    grid = (span, WIDE, LANES)
    scratch = [
        vm((4, 3) + grid, F32),
        vm((4, 3) + grid, F32),
        vm((4,) + grid, jnp.int32),
        vm((4,) + grid, F32),
        vm((4,) + grid, F32),
        vm((4, 3) + grid, F32),
        vm((4, 3) + grid, F32),
        vm((4,) + grid, F32),
        vm((9, 3, 4, rows, cols), F32),
        vm((ITERS, 12, rows + 2 * RING, WIDE, LANES), F32),
        vm((22,) + grid, F32),
        vm((ITERS, 2, 1, LANES), F32),
        vm((ITERS, n_col, LANES), F32),
        vm((ITERS, n_row, LANES), F32),
        vm((ITERS, 2, 1, LANES), F32),
        dma((3,)), dma(()),
        dma((8, 3)), dma((8, 3)),
        dma((8,)), dma((8,)),
        dma((ITERS,)), dma((ITERS,)), dma((ITERS,)), dma((ITERS,)), dma((3,)), dma((3,)),
        pltpu.SemaphoreType.REGULAR((3,)),
    ]
    return kernel, scratch


def solution(mesh):
    n_row, n_col = mesh.shape["row"], mesh.shape["col"]

    def on_device(points_here, points_there, outlier_mask, transforms):
        rows, cols = transforms.shape[2:]
        kernel, scratch = make_kernel(n_row, n_col, rows, cols)
        hbm = pl.BlockSpec(memory_space=pltpu.HBM)
        return pl.pallas_call(
            kernel,
            out_shape=(
                pltpu.VMEM(transforms.shape, F32),
                pltpu.VMEM((2, ITERS), F32),
            ),
            in_specs=[hbm] * 4,
            out_specs=(pl.BlockSpec(memory_space=pltpu.VMEM),) * 2,
            scratch_shapes=scratch,
            compiler_params=pltpu.CompilerParams(collective_id=0, has_side_effects=True),
        )(points_here, points_there, outlier_mask, transforms)

    placed = (
        P(None, None, "row", "col", None),
        P(None, None, "row", "col", None),
        P(None, "row", "col", None),
        P(None, None, "row", "col"),
    )
    return jax.shard_map(
        on_device, mesh=mesh, in_specs=placed,
        out_specs=(P(None, None, "row", "col"), P()), check_vma=False)
```
